32 devices in a mesh: rows: 8 (over y, x, core), seq: 4 (over z).
Axes of the slice: x: 2, y: 2, z: 4, core: 2. Of those that a mesh axis runs over, the one named last changes fastest.
Arguments:
- inputs_one: bfloat16 [16, 1024, 512], P('rows', 'seq'), may hold values from -6 to 6
- inputs_two: bfloat16 [16, 1024, 512], P('rows', 'seq'), may hold values from -6 to 6
- memory: bfloat16 [16, 1024, 512], P('rows', 'seq'), may hold values from -6 to 6
- target_ids: int32 [16, 1024], P('rows', 'seq'), may hold values from 0 to 4, as said below
- memory_ids: int32 [16, 1024], P('rows', 'seq'), may hold values from 0 to 4, as said below
- cotangent_one: bfloat16 [16, 1024, 512], P('rows', 'seq'), may hold values from -6 to 6
- cotangent_two: bfloat16 [16, 1024, 512], P('rows', 'seq'), may hold values from -6 to 6
- first_gain: float32 [512], replicated, may hold values from 0.25 to 1.75
- first_bias: float32 [512], replicated, may hold values from -1.75 to 1.75
- self_query: bfloat16 [512, 512], replicated, may hold values from -0.25 to 0.25
- self_key: bfloat16 [512, 512], replicated, may hold values from -0.25 to 0.25
- self_value: bfloat16 [512, 512], replicated, may hold values from -0.25 to 0.25
- self_output: bfloat16 [512, 512], replicated, may hold values from -2 to 2
- second_gain: float32 [512], replicated, may hold values from 0.25 to 1.75
- second_bias: float32 [512], replicated, may hold values from -1.75 to 1.75
- cross_query: bfloat16 [512, 512], replicated, may hold values from -0.25 to 0.25
- cross_key: bfloat16 [512, 512], replicated, may hold values from -0.25 to 0.25
- cross_value: bfloat16 [512, 512], replicated, may hold values from -0.25 to 0.25
- cross_output: bfloat16 [512, 512], replicated, may hold values from -2 to 2
- third_gain: float32 [512], replicated, may hold values from 0.25 to 1.75
- third_bias: float32 [512], replicated, may hold values from -1.75 to 1.75
- inner_weight: bfloat16 [512, 2048], replicated, may hold values from -0.25 to 0.25
- inner_bias: float32 [2048], replicated, may hold values from -3 to 3
- outer_weight: bfloat16 [2048, 512], replicated, may hold values from -0.125 to 0.125
- outer_bias: float32 [512], replicated, may hold values from -1.75 to 1.75
Outputs:
- output_one: bfloat16 [16, 1024, 512], P('rows', 'seq')
- output_two: bfloat16 [16, 1024, 512], P('rows', 'seq')
- input_grad: bfloat16 [16, 1024, 512], P('rows', 'seq')
- memory_grad: bfloat16 [16, 1024, 512], P('rows', 'seq')
- first_gain_grad: float32 [512], replicated
- first_bias_grad: float32 [512], replicated
- self_query_grad: float32 [512, 512], replicated
- self_key_grad: float32 [512, 512], replicated
- self_value_grad: float32 [512, 512], replicated
- self_output_grad: float32 [512, 512], replicated
- second_gain_grad: float32 [512], replicated
- second_bias_grad: float32 [512], replicated
- cross_query_grad: float32 [512, 512], replicated
- cross_key_grad: float32 [512, 512], replicated
- cross_value_grad: float32 [512, 512], replicated
- cross_output_grad: float32 [512, 512], replicated
- third_gain_grad: float32 [512], replicated
- third_bias_grad: float32 [512], replicated
- inner_weight_grad: float32 [512, 2048], replicated
- inner_bias_grad: float32 [2048], replicated
- outer_weight_grad: float32 [2048, 512], replicated
- outer_bias_grad: float32 [512], replicated
The draws below stay inside these ranges and needn't reach their ends.
Inputs may be any that keep to these rules, and one draw needn't show every extreme that they name: `target_ids`: each row packs 4 documents with ids 0 to 3 in order of position, each nonempty, followed by a nonempty padding run with id 4; padding tokens see only padding. `memory_ids`: each memory row packs the same 4 document ids in order of position, each nonempty, with lengths of its own, followed by a nonempty padding run with id 4.
All inputs are finite; a program needn't handle non-finite values.
Results may differ from the reference program's by a relative error of at most 0.028.
Values may be sent and summed in bfloat16 or wider, within the bound.
No kernel may reach another device: no remote copies, remote signals or barrier semaphores. Data moves between devices by JAX's collectives and lax.ppermute only.
A program may use at most 256 MiB of HBM per device.

```python
import jax
import jax.numpy as jnp
from jax import lax

D = 512
HEADS = 8
HEAD = 64
FF = 2048
GROUP = 256
ROWS_DEV = 2
DOCS = 4
LENGTH = 1024
ROWS = 16


def segment_layout(key, spanning):
    pad_key, cut_key, span_key = jax.random.split(key, 3)
    padding = jax.random.randint(pad_key, (), LENGTH // 32, LENGTH // 16)
    filled = LENGTH - padding
    window = LENGTH - LENGTH // 16 - 1
    narrow = GROUP - LENGTH // 16 - 1
    normal_cuts = 1 + jnp.sort(jax.random.permutation(cut_key, window)[:DOCS - 1])
    span_cuts = LENGTH - GROUP + 1 + jnp.sort(jax.random.permutation(span_key, narrow)[:DOCS - 1])
    cuts = jnp.where(spanning, span_cuts, normal_cuts)
    positions = jnp.arange(LENGTH)
    counted = jnp.sum((positions[:, None] >= cuts[None, :]).astype(jnp.int32), axis=1)
    return jnp.where(positions >= filled, DOCS, counted).astype(jnp.int32)


def spanning_rows(key):
    chosen = jax.random.randint(jax.random.fold_in(key, 11), (ROWS // ROWS_DEV,), 0, ROWS_DEV)
    row_index = jnp.arange(ROWS)
    return row_index % ROWS_DEV == jnp.repeat(chosen, ROWS_DEV)


def draw_target_ids(key, part):
    spanning = spanning_rows(key)
    row_keys = jax.random.split(jax.random.fold_in(key, 23), ROWS)
    return jax.vmap(segment_layout)(row_keys, spanning)


def draw_memory_ids(key, part):
    spanning = spanning_rows(key)
    row_keys = jax.random.split(jax.random.fold_in(key, 29), ROWS)
    return jax.vmap(segment_layout)(row_keys, spanning)


def steps_of(rng, extent, shards, least, largest):
    def one(dim, blocks):
        heights = jax.random.uniform(jax.random.fold_in(jax.random.fold_in(rng, 6), dim), (blocks,), jnp.float32, least / len(shards), largest / len(shards))
        return jnp.repeat(jnp.exp(heights), extent[dim] // blocks).reshape((-1,) + (1,) * (len(extent) - dim - 1))

    loudness = one(*shards[0])
    for cut in shards[1:]:
        loudness = loudness * one(*cut)
    return loudness


def gaussian(stream_key, extent, spread, limit, cuts=(), dtype=jnp.bfloat16):
    entries = jax.random.normal(stream_key, extent, jnp.float32) * spread
    if len(cuts) > 0:
        entries = steps_of(stream_key, extent, cuts, -0.22, 0.18) * entries
    return jnp.clip(entries, min=-limit, max=limit).astype(dtype)


def setup_inputs(seed: int = 0) -> dict:
    splits = jax.random.split(jax.random.key(seed), 26)
    inputs_one = gaussian(splits[0], (ROWS, LENGTH, D), 1.0, 6.0, ((0, 8), (1, 4)))
    inputs_two = gaussian(splits[1], (ROWS, LENGTH, D), 1.0, 6.0, ((0, 8), (1, 4)))
    memory = gaussian(splits[2], (ROWS, LENGTH, D), 1.0, 6.0, ((0, 8), (1, 4)))
    target_ids = draw_target_ids(jax.random.fold_in(splits[25], 71), 0)
    memory_ids = draw_memory_ids(jax.random.fold_in(splits[25], 71), 0)
    cotangent_one = gaussian(splits[5], (ROWS, LENGTH, D), 1.0, 6.0, ((0, 8), (1, 4)))
    cotangent_two = gaussian(splits[6], (ROWS, LENGTH, D), 1.0, 6.0, ((0, 8), (1, 4)))
    first_gain = jnp.clip(1.0 + 0.15 * jax.random.normal(splits[7], (D,), jnp.float32), 0.25, 1.75)
    first_bias = gaussian(splits[8], (D,), 0.3, 1.75, (), jnp.float32)
    self_query = gaussian(splits[9], (D, D), D ** -0.5, 0.25)
    self_key = gaussian(splits[10], (D, D), D ** -0.5, 0.25)
    self_value = gaussian(splits[11], (D, D), D ** -0.5, 0.25)
    self_output = gaussian(splits[12], (D, D), (max(D // 64, 1)) ** -0.5, 2.0)
    second_gain = jnp.clip(1.0 + 0.15 * jax.random.normal(splits[13], (D,), jnp.float32), 0.25, 1.75)
    second_bias = gaussian(splits[14], (D,), 0.3, 1.75, (), jnp.float32)
    cross_query = gaussian(splits[15], (D, D), D ** -0.5, 0.25)
    cross_key = gaussian(splits[16], (D, D), D ** -0.5, 0.25)
    cross_value = gaussian(splits[17], (D, D), D ** -0.5, 0.25)
    cross_output = gaussian(splits[18], (D, D), (max(D // 64, 1)) ** -0.5, 2.0)
    third_gain = jnp.clip(1.0 + 0.15 * jax.random.normal(splits[19], (D,), jnp.float32), 0.25, 1.75)
    third_bias = gaussian(splits[20], (D,), 0.3, 1.75, (), jnp.float32)
    inner_weight = gaussian(splits[21], (D, FF), D ** -0.5, 0.25)
    inner_bias = gaussian(splits[22], (FF,), 0.5, 3.0, (), jnp.float32)
    outer_weight = gaussian(splits[23], (FF, D), FF ** -0.5, 0.125)
    outer_bias = gaussian(splits[24], (D,), 0.3, 1.75, (), jnp.float32)
    return dict(inputs_one=inputs_one, inputs_two=inputs_two, memory=memory, target_ids=target_ids, memory_ids=memory_ids, cotangent_one=cotangent_one, cotangent_two=cotangent_two, first_gain=first_gain, first_bias=first_bias, self_query=self_query, self_key=self_key, self_value=self_value, self_output=self_output, second_gain=second_gain, second_bias=second_bias, cross_query=cross_query, cross_key=cross_key, cross_value=cross_value, cross_output=cross_output, third_gain=third_gain, third_bias=third_bias, inner_weight=inner_weight, inner_bias=inner_bias, outer_weight=outer_weight, outer_bias=outer_bias)


highest = lax.Precision.HIGHEST
epsilon = 1e-05
negative = -1e+30

@jax.custom_vjp
def low(v):
    return lax.optimization_barrier(v.astype(jnp.bfloat16)).astype(jnp.float32)

@jax.custom_vjp
def low_back(v):
    return v

def low_keep(v):
    return (low(v), None)

def low_pass(kept, grad):
    return (grad,)

def back_keep(v):
    return (v, None)

def back_low(kept, grad):
    return (low(grad),)
low.defvjp(low_keep, low_pass)
low_back.defvjp(back_keep, back_low)

def layer_norm(values, gain, shift):
    centered = values - lax.optimization_barrier(jnp.mean(values, axis=-1, keepdims=True))
    variance = lax.optimization_barrier(jnp.mean(centered * centered, axis=-1, keepdims=True))
    return centered * lax.rsqrt(variance + epsilon) * gain + shift

def matmul(acts, weight):
    return jnp.einsum('...d,de->...e', acts, weight, precision=highest)

def attend_row(pack):
    queries, keys, values, query_ids, key_ids = pack
    scores = low_back(jnp.einsum('qhe,khe->qhk', queries, keys, precision=highest) * HEAD ** (-0.5))
    allowed = query_ids[:, None, None] == key_ids[None, None, :]
    probs = jax.nn.softmax(jnp.where(allowed, scores, negative), axis=-1)
    return jnp.einsum('qhk,khe->qhe', low(probs), values, precision=highest)

def attention(queries, keys, values, query_ids, key_ids):
    query_shape = (queries.shape[0], queries.shape[1], HEADS, HEAD)
    key_shape = (keys.shape[0], keys.shape[1], HEADS, HEAD)
    result = lax.map(jax.checkpoint(attend_row), (queries.reshape(query_shape), keys.reshape(key_shape), values.reshape(key_shape), query_ids, key_ids))
    return result.reshape(queries.shape)

def layer(inputs, memory_keys, memory_values, target_ids, memory_ids, params):
    first_gain, first_bias, self_query, self_key, self_value, self_output, second_gain, second_bias, cross_query, cross_key, cross_value, cross_output, third_gain, third_bias, inner_weight, inner_bias, outer_weight, outer_bias = params
    normed = low(layer_norm(inputs, first_gain, first_bias))
    queries = low_back(low(matmul(normed, self_query)))
    keys = low_back(low(matmul(normed, self_key)))
    values = low_back(low(matmul(normed, self_value)))
    attended = low_back(low(attention(queries, keys, values, target_ids, target_ids)))
    middle = inputs + low_back(matmul(attended, self_output))
    normed = low(layer_norm(middle, second_gain, second_bias))
    cross_queries = low_back(low(matmul(normed, cross_query)))
    crossed = low_back(low(attention(cross_queries, memory_keys, memory_values, target_ids, memory_ids)))
    later = middle + low_back(matmul(crossed, cross_output))
    normed = low(layer_norm(later, third_gain, third_bias))
    hidden_pre = low_back(matmul(normed, inner_weight) + inner_bias)
    hidden = low(jax.nn.gelu(hidden_pre))
    return later + low_back(matmul(hidden, outer_weight) + outer_bias)

def reference(inputs_one, inputs_two, memory, target_ids, memory_ids, cotangent_one, cotangent_two, first_gain, first_bias, self_query, self_key, self_value, self_output, second_gain, second_bias, cross_query, cross_key, cross_value, cross_output, third_gain, third_bias, inner_weight, inner_bias, outer_weight, outer_bias):
    weights = tuple((argument.astype(jnp.float32) for argument in (first_gain, first_bias, self_query, self_key, self_value, self_output, second_gain, second_bias, cross_query, cross_key, cross_value, cross_output, third_gain, third_bias, inner_weight, inner_bias, outer_weight, outer_bias)))
    fixed_input = inputs_two.astype(jnp.float32)

    def forward(first_input, memory_in, *params):
        memory_keys = low_back(low(matmul(memory_in, params[9])))
        memory_values = low_back(low(matmul(memory_in, params[10])))
        first_out = layer(first_input, memory_keys, memory_values, target_ids, memory_ids, params)
        second_out = layer(fixed_input, memory_keys, memory_values, target_ids, memory_ids, params)
        return (first_out, second_out)
    outputs, pullback = jax.vjp(forward, inputs_one.astype(jnp.float32), memory.astype(jnp.float32), *weights)
    grads = pullback((cotangent_one.astype(jnp.float32), cotangent_two.astype(jnp.float32)))
    return (outputs[0].astype(jnp.bfloat16), outputs[1].astype(jnp.bfloat16), grads[0].astype(jnp.bfloat16), grads[1].astype(jnp.bfloat16), grads[2], grads[3], grads[4], grads[5], grads[6], grads[7], grads[8], grads[9], grads[10], grads[11], grads[12], grads[13], grads[14], grads[15], grads[16], grads[17], grads[18], grads[19])
```

```python
import functools
import math

import jax
import jax.numpy as jnp
from jax import lax
from jax.experimental import pallas as pl
from jax.experimental.pallas import tpu as pltpu
from jax.sharding import PartitionSpec as P

HEADS = 8
HEAD = 64
QUAD = 4 * HEAD
epsilon = 1e-05
negative = -1e30
BOTH = ("rows", "seq")
bf16 = jnp.bfloat16
f32 = jnp.float32
LN2 = math.log(2.0)
QUERY_SCALE = HEAD ** (-0.5) / LN2
NN = ((1,), (0,))
NT = ((1,), (1,))
TN = ((0,), (0,))
GELU_A = math.sqrt(2.0 / math.pi)
GELU_B = 0.044715


def dot(left, right, dims):
    return lax.dot_general(left, right, (dims, ((), ())), preferred_element_type=f32)


def normalize(values):
    centered = values - jnp.mean(values, axis=-1, keepdims=True)
    scale = lax.rsqrt(jnp.mean(centered * centered, axis=-1, keepdims=True) + epsilon)
    return centered * scale, scale


def norm_back(normal, scale, gain, grad):
    inner = grad * gain
    mean = jnp.mean(inner, axis=-1, keepdims=True)
    along = jnp.mean(inner * normal, axis=-1, keepdims=True)
    return scale * (inner - mean - normal * along)


def mask_bias(row_ids, column_ids):
    rows = row_ids.shape[1]
    columns = column_ids.shape[1]
    spread = jnp.transpose(jnp.broadcast_to(row_ids.astype(f32), (128, rows)))
    spread = jnp.concatenate([spread] * (columns // 128), axis=1)
    return jnp.where(spread == column_ids.astype(f32), 0.0, negative)


def attend(q_ref, k_ref, v_ref, bias_ref, out_ref, lse_ref):
    count = q_ref.shape[0]
    lane = lax.broadcasted_iota(jnp.int32, (count, QUAD), 1) // HEAD
    slot = lax.broadcasted_iota(jnp.int32, (count, 128), 1)
    lse = jnp.zeros((count, 128), f32)
    for quad in range(HEADS // 4):
        span = slice(QUAD * quad, QUAD * quad + QUAD)
        queries = q_ref[:, span]
        keys = k_ref[:, span]
        values = v_ref[:, span]
        gathered = jnp.zeros((count, QUAD), f32)
        for head in range(4):
            own = jnp.where(lane == head, queries, jnp.zeros_like(queries))
            scores = dot(own, keys, NT) + bias_ref[...]
            top = jnp.max(scores, axis=1, keepdims=True)
            weights = jnp.exp2(scores - top)
            total = jnp.sum(weights, axis=1, keepdims=True)
            result = dot(weights.astype(bf16), values, NN) / total
            gathered = jnp.where(lane == head, result, gathered)
            lse = jnp.where(slot == 4 * quad + head, top + jnp.log2(total), lse)
        out_ref[:, span] = gathered.astype(bf16)
    lse_ref[...] = jnp.transpose(lse)[:HEADS]


def attend_back(q_ref, k_ref, v_ref, o_ref, lse_ref, bias_ref, do_ref, dqt_ref, take):
    count = q_ref.shape[0]
    lane = lax.broadcasted_iota(jnp.int32, (count, QUAD), 1) // HEAD
    product = do_ref[...].astype(f32) * o_ref[...].astype(f32)
    delta = jnp.sum(jnp.transpose(product).reshape(HEADS, HEAD, count), axis=1)
    for quad in range(HEADS // 4):
        span = slice(QUAD * quad, QUAD * quad + QUAD)
        queries = q_ref[:, span]
        keys = k_ref[:, span]
        values = v_ref[:, span]
        grads = do_ref[:, span]
        keys_t = jnp.transpose(keys)
        key_grad = jnp.zeros((keys.shape[0], QUAD), f32)
        value_grad = jnp.zeros((keys.shape[0], QUAD), f32)
        for head in range(4):
            index = 4 * quad + head
            own_q = jnp.where(lane == head, queries, jnp.zeros_like(queries))
            own_g = jnp.where(lane == head, grads, jnp.zeros_like(grads))
            scores = dot(keys, own_q, NT) + bias_ref[...]
            probs = jnp.exp2(scores - lse_ref[index : index + 1, :])
            value_grad = value_grad + dot(probs.astype(bf16), own_g, NN)
            prob_grad = dot(values, own_g, NT)
            score_grad = (probs * (prob_grad - delta[index : index + 1, :])).astype(bf16)
            key_grad = key_grad + dot(score_grad, own_q, NN)
            rows = slice(HEAD * index, HEAD * index + HEAD)
            part = dot(keys_t[HEAD * head : HEAD * head + HEAD], score_grad, NN)
            dqt_ref[rows, :] = (part * HEAD ** (-0.5)).astype(bf16)
        take(span, key_grad * LN2, value_grad)


def self_forward(pieces, *refs):
    xs = refs[:pieces]
    ids, gain, shift, wq, wk, wv, wo, gain_two, shift_two, wcq = refs[pieces : pieces + 10]
    n1, q, k, v, o, lse, mid, qc, bias = refs[pieces + 10 :]
    count = q.shape[0]
    group = xs[0].shape[0]
    for index, part in enumerate(xs):
        normal, _ = normalize(part[...].astype(f32))
        n1[index * group : (index + 1) * group, :] = (normal * gain[...] + shift[...]).astype(bf16)
    bias[...] = mask_bias(ids[:, :count], ids[...])
    k[...] = dot(n1[...], wk[...], NN).astype(bf16)
    v[...] = dot(n1[...], wv[...], NN).astype(bf16)
    q[...] = (dot(n1[:count, :], wq[...], NN) * QUERY_SCALE).astype(bf16)
    attend(q, k, v, bias, o, lse)
    own = jnp.concatenate([part[...] for part in xs[: count // group]], axis=0).astype(f32)
    middle = own + dot(o[...], wo[...], NN)
    mid[...] = middle
    normal, _ = normalize(middle)
    low = (normal * gain_two[...] + shift_two[...]).astype(bf16)
    qc[...] = (dot(low, wcq[...], NN) * QUERY_SCALE).astype(bf16)


def memory_project(pieces, *refs):
    ms = refs[:pieces]
    wk, wv, k, v = refs[pieces:]
    group = ms[0].shape[0]
    for index, part in enumerate(ms):
        rows = slice(index * group, (index + 1) * group)
        k[rows, :] = dot(part[...], wk[...], NN).astype(bf16)
        v[rows, :] = dot(part[...], wv[...], NN).astype(bf16)


def cross_forward(ids_q, ids_k, q, k, v, mid, wo, o, lse, later, bias):
    bias[...] = mask_bias(ids_q[...], ids_k[...])
    attend(q, k, v, bias, o, lse)
    later[...] = mid[...] + dot(o[...], wo[...], NN)


def feed_forward(later_a, later_b, cot_a, cot_b, gain, shift, win, bin_, wout, bout, out_a, out_b, grad_a, grad_b, packed, vecs, cot, acc, dnorm):
    count = later_a.shape[0]
    width = later_a.shape[1]
    inner = win.shape[1]
    cot[:count, :] = cot_a[...]
    cot[count:, :] = cot_b[...]
    later = jnp.concatenate([later_a[...], later_b[...]], axis=0)
    normal, scale = normalize(later)
    low = (normal * gain[...] + shift[...]).astype(bf16)
    bias_rows = []
    for index in range(inner // width):
        span = slice(index * width, (index + 1) * width)
        pre = dot(low, win[:, span], NN) + bin_[:, span]
        square = pre * pre
        tanh = jnp.tanh(GELU_A * (pre + GELU_B * (pre * square)))
        half = 0.5 * (1.0 + tanh)
        hidden = (pre * half).astype(bf16)
        slope = half + 0.5 * pre * (1.0 - tanh * tanh) * (GELU_A + (3.0 * GELU_A * GELU_B) * square)
        step = dot(hidden, wout[span, :], NN)
        hidden_grad = dot(cot[...], wout[span, :], NT)
        pre_grad = hidden_grad * slope
        pre_low = pre_grad.astype(bf16)
        bias_rows.append(jnp.sum(pre_grad, axis=0, keepdims=True))
        packed[index * width : (index + 1) * width, :] = dot(low, pre_low, TN).astype(bf16)
        packed[inner + index * width : inner + (index + 1) * width, :] = dot(hidden, cot[...], TN).astype(bf16)
        back = dot(pre_low, win[:, span], NT)
        if index == 0:
            acc[...] = step
            dnorm[...] = back
        else:
            acc[...] = acc[...] + step
            dnorm[...] = dnorm[...] + back
    result = (later + acc[...] + bout[...]).astype(bf16)
    out_a[...] = result[:count]
    out_b[...] = result[count:]
    dn = dnorm[...]
    cots = cot[...].astype(f32)
    grad = cots + norm_back(normal, scale, gain[...], dn)
    grad_a[...] = grad[:count]
    grad_b[...] = grad[count:]
    rows = [
        jnp.sum(dn * normal, axis=0, keepdims=True),
        jnp.sum(dn, axis=0, keepdims=True),
        jnp.sum(cots, axis=0, keepdims=True),
    ] + bias_rows
    rows.append(jnp.zeros((16 - len(rows), width), f32))
    vecs[...] = jnp.concatenate(rows, axis=0)


def cross_backward(pieces, others, *refs):
    ms = refs[:pieces]
    (
        grad_a, grad_b, mid_a, mid_b, oc_a, oc_b, qc_a, qc_b, lse_a, lse_b, os_a, os_b,
        k, v, ids_q, ids_k, wco, wcq, wck, wcv, gain, shift, vecs_in,
    ) = refs[pieces : pieces + 23]
    mg_a, mg_b, packed, mem_own, mem_other, bias, do, dqt, dk, dv = refs[pieces + 23 :]
    width = k.shape[1]
    count = qc_a.shape[0]
    group = ms[0].shape[0]
    bias[...] = mask_bias(ids_k[...], ids_q[...])
    sums = [0.0, 0.0, 0.0]
    gain_row = 0.0
    shift_row = 0.0
    steps = ((grad_a, mid_a, oc_a, qc_a, lse_a, os_a, mg_a), (grad_b, mid_b, oc_b, qc_b, lse_b, os_b, mg_b))
    for index, (grad, mid, oc, qc, lse, os_, mg) in enumerate(steps):
        branch = grad[...].astype(bf16)
        do[...] = dot(branch, wco[...], NT).astype(bf16)

        def take(span, key_grad, value_grad, first=index == 0):
            if first:
                dk[:, span] = key_grad
                dv[:, span] = value_grad
            else:
                dk[:, span] = dk[:, span] + key_grad
                dv[:, span] = dv[:, span] + value_grad

        attend_back(qc, k, v, oc, lse, bias, do, dqt, take)
        dq = jnp.transpose(dqt[...])
        normal, scale = normalize(mid[...])
        low = (normal * gain[...] + shift[...]).astype(bf16)
        dn = dot(dq, wcq[...], NT)
        middle_grad = grad[...] + norm_back(normal, scale, gain[...], dn)
        mg[...] = middle_grad
        sums[0] = sums[0] + dot(oc[...], branch, TN)
        sums[1] = sums[1] + dot(low, dq, TN)
        sums[2] = sums[2] + dot(os_[...], middle_grad.astype(bf16), TN)
        gain_row = gain_row + jnp.sum(dn * normal, axis=0, keepdims=True)
        shift_row = shift_row + jnp.sum(dn, axis=0, keepdims=True)
    dk_low = dk[...].astype(bf16)
    dv_low = dv[...].astype(bf16)
    grad_k = 0.0
    grad_v = 0.0
    for index, part in enumerate(ms):
        rows = slice(index * group, (index + 1) * group)
        grad_k = grad_k + dot(part[...], dk_low[rows], TN)
        grad_v = grad_v + dot(part[...], dv_low[rows], TN)
    for index, value in enumerate(sums + [grad_k, grad_v]):
        packed[index * width : (index + 1) * width, :] = value.astype(bf16)
    packed[5 * width :, :] = jnp.zeros((packed.shape[0] - 5 * width, width), bf16)
    rows = jnp.concatenate([vecs_in[:7, :], gain_row, shift_row, vecs_in[9:, :]], axis=0)
    packed[5 * width : 5 * width + 16, :] = rows.astype(bf16)
    mem_own[...] = dot(dk_low[:count], wck[...], NT) + dot(dv_low[:count], wcv[...], NT)
    if others:
        mem_other[...] = (dot(dk_low[count:], wck[...], NT) + dot(dv_low[count:], wcv[...], NT)).astype(bf16)


def self_backward(pieces, last, *refs):
    xs = refs[:pieces]
    mg, wo, o, q, k, v, lse, ids, n1, wq, wk, wv = refs[pieces : pieces + 12]
    rest = refs[pieces + 12 :]
    if last:
        sums_in, vecs_in, packed, bias, do, dqt, dk, dv = rest
    else:
        sums, vecs, ng_own, ng_other, bias, do, dqt, dk, dv = rest
    width = q.shape[1]
    count = q.shape[0]
    group = xs[0].shape[0]
    bias[...] = mask_bias(ids[...], ids[:, :count])
    do[...] = dot(mg[...].astype(bf16), wo[...], NT).astype(bf16)

    def take(span, key_grad, value_grad):
        dk[:, span] = key_grad.astype(bf16)
        dv[:, span] = value_grad.astype(bf16)

    attend_back(q, k, v, o, lse, bias, do, dqt, take)
    dq = jnp.transpose(dqt[...])
    grads = (dot(n1[:count, :], dq, TN), dot(n1[...], dk[...], TN), dot(n1[...], dv[...], TN))
    gain_row = 0.0
    shift_row = 0.0
    for index, part in enumerate(xs):
        rows = slice(index * group, (index + 1) * group)
        ng = dot(dk[rows, :], wk[...], NT) + dot(dv[rows, :], wv[...], NT)
        if (index + 1) * group <= count:
            ng = ng + dot(dq[rows], wq[...], NT)
            if not last:
                ng_own[rows, :] = ng
        elif not last:
            ng_other[index * group - count : (index + 1) * group - count, :] = ng.astype(bf16)
        normal, _ = normalize(part[...].astype(f32))
        gain_row = gain_row + jnp.sum(ng * normal, axis=0, keepdims=True)
        shift_row = shift_row + jnp.sum(ng, axis=0, keepdims=True)
    rows = jnp.concatenate([gain_row, shift_row, jnp.zeros((14, width), f32)], axis=0)
    if last:
        for index, value in enumerate(grads):
            span = slice(index * width, (index + 1) * width)
            packed[span, :] = (value + sums_in[span, :]).astype(bf16)
        packed[3 * width :, :] = jnp.zeros((packed.shape[0] - 3 * width, width), bf16)
        packed[3 * width : 3 * width + 16, :] = (rows + vecs_in[...]).astype(bf16)
    else:
        for index, value in enumerate(grads):
            sums[index * width : (index + 1) * width, :] = value
        vecs[...] = rows


def input_backward(parts, xa, xb, mg, ng, gain, *refs):
    received = refs[:parts]
    out = refs[parts]
    group = xa.shape[0]
    count = mg.shape[0]
    grad = ng[...]
    for index, part in enumerate(received):
        grad = grad + part[...].astype(f32)
    x = jnp.concatenate([xa[...], xb[...]], axis=0).astype(f32)
    normal, scale = normalize(x)
    out[...] = (mg[...] + norm_back(normal, scale, gain[...], grad)).astype(bf16)


def call(body, outs, args, scratch=(), flops=0, name=None):
    moved = sum(math.prod(a.shape) * a.dtype.itemsize for a in args)
    moved += sum(math.prod(s) * jnp.dtype(d).itemsize for s, d in outs)
    return pl.pallas_call(
        body,
        out_shape=[jax.ShapeDtypeStruct(s, d) for s, d in outs],
        scratch_shapes=[pltpu.VMEM(s, d) for s, d in scratch],
        compiler_params=pltpu.CompilerParams(vmem_limit_bytes=58 * 2**20),
        cost_estimate=pl.CostEstimate(flops=int(flops), bytes_accessed=int(moved), transcendentals=0),
        name=name,
    )(*args)


def local(
    inputs_one,
    inputs_two,
    memory,
    target_ids,
    memory_ids,
    cotangent_one,
    cotangent_two,
    first_gain,
    first_bias,
    self_query,
    self_key,
    self_value,
    self_output,
    second_gain,
    second_bias,
    cross_query,
    cross_key,
    cross_value,
    cross_output,
    third_gain,
    third_bias,
    inner_weight,
    inner_bias,
    outer_weight,
    outer_bias,
):
    ring = lax.axis_size("seq")
    pairs = lax.axis_size("rows") // 2
    place = lax.axis_index("seq")
    held = inputs_one.shape[0]
    group = inputs_one.shape[1]
    width = inputs_one.shape[2]
    inner = inner_weight.shape[1]
    workers = ring // held
    count = 2 * group
    length = workers * count
    pieces = 2 * workers
    others = workers - 1
    odd = place % 2

    def flat(pair, member):
        return (2 * pair + member % 2) * ring + member // 2

    def dealt(swap):
        links = []
        for pair in range(pairs):
            for core in range(2):
                for spot in range(ring):
                    row = held * core + (spot + swap) % 2
                    links.append((flat(pair, 2 * spot + core), flat(pair, row * workers + spot // 2)))
        return links

    def turned(shift):
        links = []
        for pair in range(pairs):
            for member in range(2 * ring):
                row, worker = divmod(member, workers)
                links.append((flat(pair, row * workers + (worker + shift) % workers), flat(pair, member)))
        return links

    def reverse(links):
        return [(b, a) for a, b in links]

    def send(value, links):
        return lax.ppermute(value, BOTH, links)

    def deal(value):
        first = lax.dynamic_index_in_dim(value, odd, 0, keepdims=False)
        second = lax.dynamic_index_in_dim(value, 1 - odd, 0, keepdims=False)
        return [send(first, dealt(0)), send(second, dealt(1))]

    def row_of(parts):
        whole = list(parts)
        for shift in range(1, workers):
            whole += [send(part, turned(shift)) for part in parts]
        return whole

    def undeal(value):
        first = send(value[:group], reverse(dealt(0)))
        second = send(value[group:], reverse(dealt(1)))
        even = jnp.stack([first, second])
        return jnp.where(odd == 0, even, even[::-1])

    def back_sum(own, rest):
        return [
            send(rest[(shift - 1) * count : shift * count], reverse(turned(shift))) for shift in range(1, workers)
        ]

    def row(vector):
        return vector.reshape(1, -1)

    g1, b1, g2, b2, g3, b3 = map(
        row, (first_gain, first_bias, second_gain, second_bias, third_gain, third_bias)
    )
    ids = row_of(deal(jnp.stack([target_ids, memory_ids], axis=1)))
    ids = jnp.concatenate(ids, axis=1)
    ids_t = ids[:1]
    ids_m = ids[1:]
    ids_q = ids_t[:, :count]

    own_one = deal(inputs_one)
    x_one = row_of(own_one)
    memory, inputs_two, own_one = lax.optimization_barrier((memory, inputs_two, own_one))
    own_memory = deal(memory)
    own_two = deal(inputs_two)
    mem = row_of(own_memory)
    x_two = row_of(own_two)
    cotangent_one, cotangent_two, own_two, own_memory = lax.optimization_barrier(
        (cotangent_one, cotangent_two, own_two, own_memory)
    )
    cot_one = jnp.concatenate(deal(cotangent_one), axis=0)
    cot_two = jnp.concatenate(deal(cotangent_two), axis=0)

    tokens = (count, width)
    whole = (length, width)
    lse = (HEADS, count)
    scores = 2 * count * length * width
    square = 2 * count * width * width

    def run_self(xs):
        return call(
            functools.partial(self_forward, pieces),
            [(whole, bf16), (tokens, bf16), (whole, bf16), (whole, bf16), (tokens, bf16), (lse, f32), (tokens, f32), (tokens, bf16)],
            [*xs, ids_t, g1, b1, self_query, self_key, self_value, self_output, g2, b2, cross_query],
            [((count, length), f32)],
            8 * scores + (3 + 2 * workers) * square,
            "self_forward",
        )

    def run_cross(qc, mid):
        return call(
            cross_forward,
            [(tokens, bf16), (lse, f32), (tokens, f32)],
            [ids_q, ids_m, qc, mem_k, mem_v, mid, cross_output],
            [((count, length), f32)],
            8 * scores + square,
            "cross_forward",
        )

    n1_a, q_a, k_a, v_a, o_a, lse_a, mid_a, qc_a = run_self(x_one)
    mem_k, mem_v = call(
        functools.partial(memory_project, pieces),
        [(whole, bf16), (whole, bf16)],
        [*mem, cross_key, cross_value],
        flops=2 * workers * square,
        name="memory_project",
    )
    oc_a, lsec_a, later_a = run_cross(qc_a, mid_a)
    n1_b, q_b, k_b, v_b, o_b, lse_b, mid_b, qc_b = run_self(x_two)
    oc_b, lsec_b, later_b = run_cross(qc_b, mid_b)
    both = (2 * count, width)
    out_a, out_b, lg_a, lg_b, packed_ff, vecs = call(
        feed_forward,
        [(tokens, bf16), (tokens, bf16), (tokens, f32), (tokens, f32), ((2 * inner, width), bf16), ((16, width), f32)],
        [later_a, later_b, cot_one, cot_two, g3, b3, inner_weight, row(inner_bias), outer_weight, row(outer_bias)],
        [(both, bf16), (both, f32), (both, f32)],
        2 * 6 * square * inner // width,
        "feed_forward",
    )
    rest = (max(others, 1) * count, width)
    mg_a, mg_b, packed_cross, mem_own, mem_other = call(
        functools.partial(cross_backward, pieces, others),
        [(tokens, f32), (tokens, f32), ((6 * width, width), bf16), (tokens, f32), (rest, bf16)],
        [
            *mem, lg_a, lg_b, mid_a, mid_b, oc_a, oc_b, qc_a, qc_b, lsec_a, lsec_b, o_a, o_b,
            mem_k, mem_v, ids_q, ids_m, cross_output, cross_query, cross_key, cross_value, g2, b2, vecs,
        ],
        [((length, count), f32), (tokens, bf16), ((width, count), bf16), (whole, f32), (whole, f32)],
        2 * 20 * scores + 14 * square,
        "cross_backward",
    )
    back_scratch = [((length, count), f32), (tokens, bf16), ((width, count), bf16), (whole, bf16), (whole, bf16)]
    sums, vecs_self, ng_own, ng_other = call(
        functools.partial(self_backward, pieces, False),
        [((3 * width, width), f32), ((16, width), f32), (tokens, f32), (rest, bf16)],
        [*x_one, mg_a, self_output, o_a, q_a, k_a, v_a, lse_a, ids_t, n1_a, self_query, self_key, self_value],
        back_scratch,
        20 * scores + 11 * square,
        "self_backward",
    )
    received = back_sum(ng_own, ng_other)
    input_grad = call(
        functools.partial(input_backward, others),
        [(tokens, bf16)],
        [*own_one, mg_a, ng_own, g1, *received],
        name="input_backward",
    )[0]
    packed_self = call(
        functools.partial(self_backward, pieces, True),
        [((4 * width, width), bf16)],
        [*x_two, mg_b, self_output, o_b, q_b, k_b, v_b, lse_b, ids_t, n1_b, self_query, self_key, self_value, sums, vecs_self],
        back_scratch,
        20 * scores + 11 * square,
        "self_backward_last",
    )[0]
    memory_sum = mem_own
    for part in back_sum(mem_own, mem_other):
        memory_sum = memory_sum + part.astype(f32)

    packed_ff = lax.psum(packed_ff, BOTH)
    packed_cross = lax.psum(packed_cross, BOTH)
    packed_self = lax.psum(packed_self, BOTH)

    def block(packed, index):
        return packed[index * width : (index + 1) * width].astype(f32)

    vec = packed_cross[5 * width : 5 * width + 16].astype(f32)
    vec_self = packed_self[3 * width : 3 * width + 2].astype(f32)
    inner_grad = jnp.concatenate([block(packed_ff, i) for i in range(inner // width)], axis=1)
    outer_grad = packed_ff[inner:].astype(f32)
    return (
        undeal(out_a),
        undeal(out_b),
        undeal(input_grad),
        undeal(memory_sum.astype(bf16)),
        vec_self[0],
        vec_self[1],
        block(packed_self, 0),
        block(packed_self, 1),
        block(packed_self, 2),
        block(packed_cross, 2),
        vec[7],
        vec[8],
        block(packed_cross, 1),
        block(packed_cross, 3),
        block(packed_cross, 4),
        block(packed_cross, 0),
        vec[0],
        vec[1],
        inner_grad,
        vec[3 : 3 + inner // width].reshape(-1),
        outer_grad,
        vec[2],
    )


def solution(mesh):
    split = P("rows", "seq", None)
    ids = P("rows", "seq")
    return jax.shard_map(
        local,
        mesh=mesh,
        in_specs=(split, split, split, ids, ids, split, split) + (P(),) * 18,
        out_specs=(split,) * 4 + (P(),) * 18,
        check_vma=False,
    )
```

```python
import functools
import math

import jax
import jax.numpy as jnp
from jax import lax
from jax.experimental import pallas as pl
from jax.experimental.pallas import tpu as pltpu
from jax.sharding import PartitionSpec as P

HEADS = 8
HEAD = 64
QUAD = 4 * HEAD
epsilon = 1e-05
negative = -1e30
BOTH = ("rows", "seq")
bf16 = jnp.bfloat16
f32 = jnp.float32
LN2 = math.log(2.0)
QUERY_SCALE = HEAD ** (-0.5) / LN2
NN = ((1,), (0,))
NT = ((1,), (1,))
TN = ((0,), (0,))
GELU_A = math.sqrt(2.0 / math.pi)
GELU_B = 0.044715


def dot(left, right, dims):
    return lax.dot_general(left, right, (dims, ((), ())), preferred_element_type=f32)


def normalize(values):
    centered = values - jnp.mean(values, axis=-1, keepdims=True)
    scale = lax.rsqrt(jnp.mean(centered * centered, axis=-1, keepdims=True) + epsilon)
    return centered * scale, scale


def norm_back(normal, scale, gain, grad):
    inner = grad * gain
    mean = jnp.mean(inner, axis=-1, keepdims=True)
    along = jnp.mean(inner * normal, axis=-1, keepdims=True)
    return scale * (inner - mean - normal * along)


def mask_bias(row_ids, column_ids):
    rows = row_ids.shape[1]
    columns = column_ids.shape[1]
    spread = jnp.transpose(jnp.broadcast_to(row_ids.astype(f32), (128, rows)))
    spread = jnp.concatenate([spread] * (columns // 128), axis=1)
    return jnp.where(spread == column_ids.astype(f32), 0.0, negative)


def attend(q_ref, k_ref, v_ref, bias_ref, out_ref, lse_ref):
    count = q_ref.shape[0]
    lane = lax.broadcasted_iota(jnp.int32, (count, QUAD), 1) // HEAD
    slot = lax.broadcasted_iota(jnp.int32, (count, 128), 1)
    lse = jnp.zeros((count, 128), f32)
    for quad in range(HEADS // 4):
        span = slice(QUAD * quad, QUAD * quad + QUAD)
        queries = q_ref[:, span]
        keys = k_ref[:, span]
        values = v_ref[:, span]
        gathered = jnp.zeros((count, QUAD), f32)
        for head in range(4):
            own = jnp.where(lane == head, queries, jnp.zeros_like(queries))
            scores = dot(own, keys, NT) + bias_ref[...]
            top = jnp.max(scores, axis=1, keepdims=True)
            weights = jnp.exp2(scores - top)
            total = jnp.sum(weights, axis=1, keepdims=True)
            result = dot(weights.astype(bf16), values, NN) / total
            gathered = jnp.where(lane == head, result, gathered)
            lse = jnp.where(slot == 4 * quad + head, top + jnp.log2(total), lse)
        out_ref[:, span] = gathered.astype(bf16)
    lse_ref[...] = jnp.transpose(lse)[:HEADS]


def attend_back(q_ref, k_ref, v_ref, o_ref, lse_ref, bias_ref, do_ref, dqt_ref, take):
    count = q_ref.shape[0]
    lane = lax.broadcasted_iota(jnp.int32, (count, QUAD), 1) // HEAD
    product = do_ref[...].astype(f32) * o_ref[...].astype(f32)
    delta = jnp.sum(jnp.transpose(product).reshape(HEADS, HEAD, count), axis=1)
    for quad in range(HEADS // 4):
        span = slice(QUAD * quad, QUAD * quad + QUAD)
        queries = q_ref[:, span]
        keys = k_ref[:, span]
        values = v_ref[:, span]
        grads = do_ref[:, span]
        keys_t = jnp.transpose(keys)
        key_grad = jnp.zeros((keys.shape[0], QUAD), f32)
        value_grad = jnp.zeros((keys.shape[0], QUAD), f32)
        for head in range(4):
            index = 4 * quad + head
            own_q = jnp.where(lane == head, queries, jnp.zeros_like(queries))
            own_g = jnp.where(lane == head, grads, jnp.zeros_like(grads))
            scores = dot(keys, own_q, NT) + bias_ref[...]
            probs = jnp.exp2(scores - lse_ref[index : index + 1, :])
            value_grad = value_grad + dot(probs.astype(bf16), own_g, NN)
            prob_grad = dot(values, own_g, NT)
            score_grad = (probs * (prob_grad - delta[index : index + 1, :])).astype(bf16)
            key_grad = key_grad + dot(score_grad, own_q, NN)
            rows = slice(HEAD * index, HEAD * index + HEAD)
            part = dot(keys_t[HEAD * head : HEAD * head + HEAD], score_grad, NN)
            dqt_ref[rows, :] = (part * HEAD ** (-0.5)).astype(bf16)
        take(span, key_grad * LN2, value_grad)


def token_parts(refs, step, group):
    return [ref.at[step * group : (step + 1) * group, :] for ref in refs]


def self_forward(pieces, step, *refs):
    gain, shift, wq, wk, wv, wo, gain_two, shift_two, wcq = refs[pieces : pieces + 9]
    n1, q, k, v, o, lse, mid, qc, ids, ids_m, bias = refs[pieces + 9 :]
    count = q.shape[0]
    group = count // 2
    xs = token_parts(refs[:pieces], step, group)
    for index, ref in enumerate(refs[:pieces]):
        row = ref[2 * group : 2 * group + 1, :].astype(f32)
        ids[:, index * group : (index + 1) * group] = row[:, :group]
        ids_m[:, index * group : (index + 1) * group] = row[:, group : 2 * group]
    for index, part in enumerate(xs):
        normal, _ = normalize(part[...].astype(f32))
        n1[index * group : (index + 1) * group, :] = (normal * gain[...] + shift[...]).astype(bf16)
    bias[...] = mask_bias(ids[:, :count], ids[...])
    k[...] = dot(n1[...], wk[...], NN).astype(bf16)
    v[...] = dot(n1[...], wv[...], NN).astype(bf16)
    q[...] = (dot(n1[:count, :], wq[...], NN) * QUERY_SCALE).astype(bf16)
    attend(q, k, v, bias, o, lse)
    own = jnp.concatenate([part[...] for part in xs[: count // group]], axis=0).astype(f32)
    middle = own + dot(o[...], wo[...], NN)
    mid[...] = middle
    normal, _ = normalize(middle)
    low = (normal * gain_two[...] + shift_two[...]).astype(bf16)
    qc[...] = (dot(low, wcq[...], NN) * QUERY_SCALE).astype(bf16)


def memory_project(pieces, *refs):
    ms = refs[:pieces]
    wk, wv, k, v = refs[pieces:]
    group = ms[0].shape[0]
    for index, part in enumerate(ms):
        rows = slice(index * group, (index + 1) * group)
        k[rows, :] = dot(part[...], wk[...], NN).astype(bf16)
        v[rows, :] = dot(part[...], wv[...], NN).astype(bf16)


def cross_forward(ids_q, ids_k, q, k, v, mid, wo, o, lse, later, bias):
    bias[...] = mask_bias(ids_q[:, : q.shape[0]], ids_k[...])
    attend(q, k, v, bias, o, lse)
    later[...] = mid[...] + dot(o[...], wo[...], NN)


def feed_forward(later_a, later_b, cot_a, cot_b, gain, shift, win, bin_, wout, bout, out_a, out_b, grad_a, grad_b, packed, vecs, cot, acc, dnorm):
    count = later_a.shape[0]
    width = later_a.shape[1]
    inner = win.shape[1]
    group = count // 2
    for step in range(2):
        for half, part in enumerate((cot_a, cot_b)):
            start = (2 * step + half) * group
            cot[start : start + group, :] = part[step * group : (step + 1) * group, :]
    later = jnp.concatenate([later_a[...], later_b[...]], axis=0)
    normal, scale = normalize(later)
    low = (normal * gain[...] + shift[...]).astype(bf16)
    bias_rows = []
    for index in range(inner // width):
        span = slice(index * width, (index + 1) * width)
        pre = dot(low, win[:, span], NN) + bin_[:, span]
        square = pre * pre
        tanh = jnp.tanh(GELU_A * (pre + GELU_B * (pre * square)))
        half = 0.5 * (1.0 + tanh)
        hidden = (pre * half).astype(bf16)
        slope = half + 0.5 * pre * (1.0 - tanh * tanh) * (GELU_A + (3.0 * GELU_A * GELU_B) * square)
        step = dot(hidden, wout[span, :], NN)
        hidden_grad = dot(cot[...], wout[span, :], NT)
        pre_grad = hidden_grad * slope
        pre_low = pre_grad.astype(bf16)
        bias_rows.append(jnp.sum(pre_grad, axis=0, keepdims=True))
        packed[:, span] = dot(low, pre_low, TN).astype(bf16)
        packed[:, inner + index * width : inner + (index + 1) * width] = dot(hidden, cot[...], TN).astype(bf16)
        back = dot(pre_low, win[:, span], NT)
        if index == 0:
            acc[...] = step
            dnorm[...] = back
        else:
            acc[...] = acc[...] + step
            dnorm[...] = dnorm[...] + back
    result = (later + acc[...] + bout[...]).astype(bf16)
    for half, out in enumerate((out_a, out_b)):
        for step in range(2):
            start = (2 * step + half) * group
            out[step * group : (step + 1) * group, :] = result[start : start + group]
    dn = dnorm[...]
    cots = cot[...].astype(f32)
    grad = cots + norm_back(normal, scale, gain[...], dn)
    grad_a[...] = grad[:count]
    grad_b[...] = grad[count:]
    rows = [
        jnp.sum(dn * normal, axis=0, keepdims=True),
        jnp.sum(dn, axis=0, keepdims=True),
        jnp.sum(cots, axis=0, keepdims=True),
    ] + bias_rows
    rows.append(jnp.zeros((16 - len(rows), width), f32))
    vecs[...] = jnp.concatenate(rows, axis=0)


def put_vectors(packed, start, rows):
    packed[:, start : start + 128] = jnp.zeros((packed.shape[0], 128), bf16)
    for block in range(rows.shape[1] // 128):
        part = rows[:, 128 * block : 128 * block + 128]
        packed[16 * block : 16 * block + 16, start : start + 128] = part.astype(bf16)


def cross_backward(pieces, others, *refs):
    ms = refs[:pieces]
    (
        grad_a, grad_b, mid_a, mid_b, oc_a, oc_b, qc_a, qc_b, lse_a, lse_b, os_a, os_b,
        k, v, ids_q, ids_k, wco, wcq, wck, wcv, gain, shift, vecs_in,
    ) = refs[pieces : pieces + 23]
    mg_a, mg_b, packed, mem_own, mem_other, bias, do, dqt, dk, dv = refs[pieces + 23 :]
    width = k.shape[1]
    count = qc_a.shape[0]
    group = ms[0].shape[0]
    bias[...] = mask_bias(ids_k[...], ids_q[:, :count])
    sums = [0.0, 0.0, 0.0]
    gain_row = 0.0
    shift_row = 0.0
    steps = ((grad_a, mid_a, oc_a, qc_a, lse_a, os_a, mg_a), (grad_b, mid_b, oc_b, qc_b, lse_b, os_b, mg_b))
    for index, (grad, mid, oc, qc, lse, os_, mg) in enumerate(steps):
        branch = grad[...].astype(bf16)
        do[...] = dot(branch, wco[...], NT).astype(bf16)

        def take(span, key_grad, value_grad, first=index == 0):
            if first:
                dk[:, span] = key_grad
                dv[:, span] = value_grad
            else:
                dk[:, span] = dk[:, span] + key_grad
                dv[:, span] = dv[:, span] + value_grad

        attend_back(qc, k, v, oc, lse, bias, do, dqt, take)
        dq = jnp.transpose(dqt[...])
        normal, scale = normalize(mid[...])
        low = (normal * gain[...] + shift[...]).astype(bf16)
        dn = dot(dq, wcq[...], NT)
        middle_grad = grad[...] + norm_back(normal, scale, gain[...], dn)
        mg[...] = middle_grad
        sums[0] = sums[0] + dot(oc[...], branch, TN)
        sums[1] = sums[1] + dot(low, dq, TN)
        sums[2] = sums[2] + dot(os_[...], middle_grad.astype(bf16), TN)
        gain_row = gain_row + jnp.sum(dn * normal, axis=0, keepdims=True)
        shift_row = shift_row + jnp.sum(dn, axis=0, keepdims=True)
    dk_low = dk[...].astype(bf16)
    dv_low = dv[...].astype(bf16)
    grad_k = 0.0
    grad_v = 0.0
    for index, part in enumerate(ms):
        rows = slice(index * group, (index + 1) * group)
        grad_k = grad_k + dot(part[...], dk_low[rows], TN)
        grad_v = grad_v + dot(part[...], dv_low[rows], TN)
    for index, value in enumerate(sums + [grad_k, grad_v]):
        packed[:, index * width : (index + 1) * width] = value.astype(bf16)
    rows = jnp.concatenate([vecs_in[:7, :], gain_row, shift_row, vecs_in[9:, :]], axis=0)
    put_vectors(packed, 5 * width, rows)
    mem_own[...] = dot(dk_low[:count], wck[...], NT) + dot(dv_low[:count], wcv[...], NT)
    if others:
        mem_other[...] = (dot(dk_low[count:], wck[...], NT) + dot(dv_low[count:], wcv[...], NT)).astype(bf16)


def self_backward(pieces, step, *refs):
    last = step == 1
    mg, wo, o, q, k, v, lse, ids, n1, wq, wk, wv = refs[pieces : pieces + 12]
    rest = refs[pieces + 12 :]
    if last:
        sums_in, vecs_in, packed, bias, do, dqt, dk, dv = rest
    else:
        sums, vecs, ng_own, ng_other, bias, do, dqt, dk, dv = rest
    width = q.shape[1]
    count = q.shape[0]
    group = count // 2
    xs = token_parts(refs[:pieces], step, group)
    bias[...] = mask_bias(ids[...], ids[:, :count])
    do[...] = dot(mg[...].astype(bf16), wo[...], NT).astype(bf16)

    def take(span, key_grad, value_grad):
        dk[:, span] = key_grad.astype(bf16)
        dv[:, span] = value_grad.astype(bf16)

    attend_back(q, k, v, o, lse, bias, do, dqt, take)
    dq = jnp.transpose(dqt[...])
    grads = (dot(n1[:count, :], dq, TN), dot(n1[...], dk[...], TN), dot(n1[...], dv[...], TN))
    gain_row = 0.0
    shift_row = 0.0
    for index, part in enumerate(xs):
        rows = slice(index * group, (index + 1) * group)
        ng = dot(dk[rows, :], wk[...], NT) + dot(dv[rows, :], wv[...], NT)
        if (index + 1) * group <= count:
            ng = ng + dot(dq[rows], wq[...], NT)
            if not last:
                ng_own[rows, :] = ng
        elif not last:
            ng_other[index * group - count : (index + 1) * group - count, :] = ng.astype(bf16)
        normal, _ = normalize(part[...].astype(f32))
        gain_row = gain_row + jnp.sum(ng * normal, axis=0, keepdims=True)
        shift_row = shift_row + jnp.sum(ng, axis=0, keepdims=True)
    rows = jnp.concatenate([gain_row, shift_row, jnp.zeros((14, width), f32)], axis=0)
    if last:
        for index, value in enumerate(grads):
            span = slice(index * width, (index + 1) * width)
            packed[:, span] = (value + sums_in[span, :]).astype(bf16)
        put_vectors(packed, 3 * width, rows + vecs_in[...])
    else:
        for index, value in enumerate(grads):
            sums[index * width : (index + 1) * width, :] = value
        vecs[...] = rows


def input_backward(parts, xa, xb, mg, ng, mem_own, gain, *refs):
    received = refs[:parts]
    mem_received = refs[parts : 2 * parts]
    halves = refs[2 * parts :]
    count = mg.shape[0]
    group = count // 2
    grad = ng[...]
    memory_grad = mem_own[...]
    for part, mem_part in zip(received, mem_received):
        grad = grad + part[...].astype(f32)
        memory_grad = memory_grad + mem_part[...].astype(f32)
    x = jnp.concatenate([xa[:group, :], xb[:group, :]], axis=0).astype(f32)
    normal, scale = normalize(x)
    result = (mg[...] + norm_back(normal, scale, gain[...], grad)).astype(bf16)
    memory_grad = memory_grad.astype(bf16)
    for half, out in enumerate(halves):
        out[:group, :] = memory_grad[half * group : (half + 1) * group]
        out[group:, :] = result[half * group : (half + 1) * group]


def call(body, outs, args, scratch=(), flops=0, name=None):
    moved = sum(math.prod(a.shape) * a.dtype.itemsize for a in args)
    moved += sum(math.prod(s) * jnp.dtype(d).itemsize for s, d in outs)
    return pl.pallas_call(
        body,
        out_shape=[jax.ShapeDtypeStruct(s, d) for s, d in outs],
        scratch_shapes=[pltpu.VMEM(s, d) for s, d in scratch],
        compiler_params=pltpu.CompilerParams(vmem_limit_bytes=58 * 2**20),
        cost_estimate=pl.CostEstimate(flops=int(flops), bytes_accessed=int(moved), transcendentals=0),
        name=name,
    )(*args)


def local(
    inputs_one,
    inputs_two,
    memory,
    target_ids,
    memory_ids,
    cotangent_one,
    cotangent_two,
    first_gain,
    first_bias,
    self_query,
    self_key,
    self_value,
    self_output,
    second_gain,
    second_bias,
    cross_query,
    cross_key,
    cross_value,
    cross_output,
    third_gain,
    third_bias,
    inner_weight,
    inner_bias,
    outer_weight,
    outer_bias,
):
    ring = lax.axis_size("seq")
    pairs = lax.axis_size("rows") // 2
    place = lax.axis_index("seq")
    held = inputs_one.shape[0]
    group = inputs_one.shape[1]
    width = inputs_one.shape[2]
    inner = inner_weight.shape[1]
    workers = ring // held
    count = 2 * group
    length = workers * count
    pieces = 2 * workers
    others = workers - 1
    odd = place % 2

    def flat(pair, member):
        return (2 * pair + member % 2) * ring + member // 2

    def dealt(swap):
        links = []
        for pair in range(pairs):
            for core in range(2):
                for spot in range(ring):
                    row = held * core + (spot + swap) % 2
                    links.append((flat(pair, 2 * spot + core), flat(pair, row * workers + spot // 2)))
        return links

    def turned(shift):
        links = []
        for pair in range(pairs):
            for member in range(2 * ring):
                row, worker = divmod(member, workers)
                links.append((flat(pair, row * workers + (worker + shift) % workers), flat(pair, member)))
        return links

    def reverse(links):
        return [(b, a) for a, b in links]

    def send(value, links):
        return lax.ppermute(value, BOTH, links)

    def pick(value, swap):
        return lax.dynamic_index_in_dim(value, odd if swap == 0 else 1 - odd, 0, keepdims=False)

    def deal(*values):
        return [send(jnp.concatenate([pick(v, s) for v in values], axis=0), dealt(s)) for s in range(2)]

    def row_of(parts):
        whole = list(parts)
        for shift in range(1, workers):
            whole += [send(part, turned(shift)) for part in parts]
        return whole

    def back_sum(rest):
        return [
            send(rest[(shift - 1) * count : shift * count], reverse(turned(shift))) for shift in range(1, workers)
        ]

    def row(vector):
        return vector.reshape(1, -1)

    def give_back(halves):
        return [send(half, reverse(dealt(s))) for s, half in enumerate(halves)]

    def undeal(parts, step):
        parts = [part[step * group : (step + 1) * group] for part in parts]
        return jnp.where(odd == 0, jnp.stack(parts), jnp.stack(parts[::-1]))

    spot = lax.axis_index("rows")
    core = spot % 2
    bits = pairs.bit_length() - 1

    def chip_stage(turn):
        links = []
        for i in range(2 * pairs):
            links.append((i, i ^ (2 << ((turn + i % 2) % bits))))
        bit = jnp.where(core == 0, (spot >> (1 + turn % bits)) & 1, (spot >> (1 + (turn + 1) % bits)) & 1)
        return bit, links

    stages = [(core, [(i, i ^ 1) for i in range(2 * pairs)])] + [chip_stage(turn) for turn in range(bits)]

    def split(value, stage):
        bit, links = stages[stage]
        value = value.reshape((2, value.shape[0] // 2) + value.shape[1:])
        take = lambda i: lax.dynamic_index_in_dim(value, i, 0, keepdims=False)
        return take(bit), lax.ppermute(take(1 - bit), "rows", links)

    def total(first, *rest):
        result = first.astype(f32)
        for part in rest:
            result = result + part.astype(f32)
        return result.astype(bf16)

    def along(value, turn):
        return value, lax.ppermute(value, "seq", [(i, i ^ (1 << turn)) for i in range(ring)])

    def join(value, stage):
        bit, links = stages[stage]
        other = lax.ppermute(value, "rows", links)
        return jnp.where(bit == 0, jnp.concatenate([value, other]), jnp.concatenate([other, value]))

    turns = ring.bit_length() - 1
    direct = {
        "core": ("rows", 2, core, [[(i, i ^ 1) for i in range(2 * pairs)]]),
        "chips": ("rows", pairs, spot // 2, [[(i, i ^ (2 * k)) for i in range(2 * pairs)] for k in range(1, pairs)]),
        "line": ("seq", ring, place, [[(i, i ^ k) for i in range(ring)] for k in range(1, ring)]),
    }

    def spread(value, stage):
        axis, size, index, links = direct[stage]
        value = value.reshape((size, value.shape[0] // size) + value.shape[1:])
        take = lambda i: lax.dynamic_index_in_dim(value, i, 0, keepdims=False)
        return [take(index)] + [lax.ppermute(take(index ^ (k + 1)), axis, link) for k, link in enumerate(links)]

    def gather(value, stage):
        axis, size, index, links = direct[stage]
        parts = [value] + [lax.ppermute(value, axis, link) for link in links]
        levels = size.bit_length() - 1
        result = jnp.stack(parts).reshape((2,) * levels + value.shape)
        for level in range(levels):
            result = jnp.where((index >> level) & 1 == 1, jnp.flip(result, levels - 1 - level), result)
        return result.reshape((size * value.shape[0],) + value.shape[1:])

    def after(values, *needed):
        return lax.optimization_barrier((values, needed))[0]

    g1, b1, g2, b2, g3, b3 = map(
        row, (first_gain, first_bias, second_gain, second_bias, third_gain, third_bias)
    )
    id_block = jnp.concatenate([target_ids, memory_ids], axis=1).astype(bf16)[:, None, :]
    id_block = jnp.pad(id_block, ((0, 0), (0, 15), (0, width - 2 * group)))
    own = deal(inputs_one, inputs_two, id_block)
    xs = row_of(own)
    own_memory = deal(after(memory, *xs))

    tokens = (count, width)
    whole = (length, width)
    lse = (HEADS, count)
    scores = 2 * count * length * width
    square = 2 * count * width * width

    def run_self(xs, step):
        return call(
            functools.partial(self_forward, pieces, step),
            [
                (whole, bf16), (tokens, bf16), (whole, bf16), (whole, bf16), (tokens, bf16), (lse, f32), (tokens, f32),
                (tokens, bf16), ((1, length), f32), ((1, length), f32),
            ],
            [*xs, g1, b1, self_query, self_key, self_value, self_output, g2, b2, cross_query],
            [((count, length), f32)],
            8 * scores + (3 + 2 * workers) * square,
            "self_forward",
        )

    def run_cross(qc, mid):
        return call(
            cross_forward,
            [(tokens, bf16), (lse, f32), (tokens, f32)],
            [ids_t, ids_m, qc, mem_k, mem_v, mid, cross_output],
            [((count, length), f32)],
            8 * scores + square,
            "cross_forward",
        )

    n1_a, q_a, k_a, v_a, o_a, lse_a, mid_a, qc_a, ids_t, ids_m = run_self(xs, 0)
    n1_b, q_b, k_b, v_b, o_b, lse_b, mid_b, qc_b, _, _ = run_self(after(xs, qc_a, *own_memory), 1)
    mem = row_of(after(own_memory, qc_a))
    cots = deal(*after((cotangent_one, cotangent_two), *mem))
    mem_k, mem_v = call(
        functools.partial(memory_project, pieces),
        [(whole, bf16), (whole, bf16)],
        [*mem, cross_key, cross_value],
        flops=2 * workers * square,
        name="memory_project",
    )
    oc_a, lsec_a, later_a = run_cross(qc_a, mid_a)
    oc_b, lsec_b, later_b = run_cross(after(qc_b, oc_a), mid_b)
    both = (2 * count, width)
    out_a, out_b, lg_a, lg_b, packed_ff, vecs = call(
        feed_forward,
        [((2 * group, width), bf16), ((2 * group, width), bf16), (tokens, f32), (tokens, f32), ((width, 2 * inner), bf16), ((16, width), f32)],
        [later_a, later_b, *cots, g3, b3, inner_weight, row(inner_bias), outer_weight, row(outer_bias)],
        [(both, bf16), (both, f32), (both, f32)],
        2 * 6 * square * inner // width,
        "feed_forward",
    )
    rest = (max(others, 1) * count, width)
    back_out = give_back([out_a, out_b])
    ff_sum = lax.psum_scatter(packed_ff, "rows", scatter_dimension=0, tiled=True)
    ff_line = lax.psum(ff_sum, "seq")
    packed_ff = lax.all_gather(ff_line, "rows", axis=0, tiled=True)
    mg_a, mg_b, packed_cross, mem_own, mem_other = call(
        functools.partial(cross_backward, pieces, others),
        [(tokens, f32), (tokens, f32), ((width, 5 * width + 128), bf16), (tokens, f32), (rest, bf16)],
        [
            *mem, lg_a, lg_b, mid_a, mid_b, oc_a, oc_b, qc_a, qc_b, lsec_a, lsec_b, o_a, o_b,
            mem_k, mem_v, ids_t, ids_m, cross_output, cross_query, cross_key, cross_value, g2, b2, vecs,
        ],
        [((length, count), f32), (tokens, bf16), ((width, count), bf16), (whole, f32), (whole, f32)],
        2 * 20 * scores + 14 * square,
        "cross_backward",
    )
    back_scratch = [((length, count), f32), (tokens, bf16), ((width, count), bf16), (whole, bf16), (whole, bf16)]
    cross_parts = split(after(packed_cross, *back_out), 0)
    memory_parts = back_sum(after(mem_other, *back_out))
    mg_a = after(mg_a, *back_out)
    sums, vecs_self, ng_own, ng_other = call(
        functools.partial(self_backward, pieces, 0),
        [((3 * width, width), f32), ((16, width), f32), (tokens, f32), (rest, bf16)],
        [*xs, mg_a, self_output, o_a, q_a, k_a, v_a, lse_a, ids_t, n1_a, self_query, self_key, self_value],
        back_scratch,
        (20 * scores + 11 * square) // 4,
        "self_backward",
    )
    received = back_sum(after(ng_other, *cross_parts, *memory_parts))
    mg_b = after(mg_b, ng_own, ff_sum, *cross_parts, *memory_parts)
    cross_parts = split(total(*after(cross_parts, ng_own)), 1)
    packed_self = call(
        functools.partial(self_backward, pieces, 1),
        [((width, 3 * width + 128), bf16)],
        [*xs, mg_b, self_output, o_b, q_b, k_b, v_b, lse_b, ids_t, n1_b, self_query, self_key, self_value, sums, vecs_self],
        back_scratch,
        20 * scores + 11 * square,
        "self_backward_last",
    )[0]
    packed_self = after(packed_self, ff_line, *cross_parts, *received)
    self_parts = spread(packed_self, "core")
    cross_sum = total(*after(cross_parts, packed_self))
    halves = call(
        functools.partial(input_backward, others),
        [((2 * group, width), bf16), ((2 * group, width), bf16)],
        [*own, mg_a, after(ng_own, packed_self), mem_own, g1, *received, *memory_parts],
        name="input_backward",
    )
    for turn in range(1, bits):
        cross_sum = total(*split(cross_sum, 1 + turn))
    self_parts = spread(total(*self_parts), "chips")
    self_sum = total(*self_parts)
    back_grad = give_back(after(halves, self_sum))
    self_sum = total(*spread(self_sum, "line"))
    for turn in range(turns):
        cross_sum = total(*along(cross_sum, turn))
    self_sum = gather(self_sum, "line")
    self_sum = gather(self_sum, "chips")
    for stage in reversed(range(1 + bits)):
        cross_sum = join(cross_sum, stage)
    packed_cross = cross_sum
    packed_self = gather(self_sum, "core")
    packed_ff = after(packed_ff, packed_self)

    def block(packed, index):
        return packed[:, index * width : (index + 1) * width].astype(f32)

    def vectors(packed, start):
        rows = packed[: 16 * (width // 128), start : start + 128].astype(f32)
        return jnp.swapaxes(rows.reshape(width // 128, 16, 128), 0, 1).reshape(16, width)

    vec = vectors(packed_cross, 5 * width)
    vec_self = vectors(packed_self, 3 * width)
    inner_grad = packed_ff[:, :inner].astype(f32)
    outer_grad = jnp.concatenate([block(packed_ff, inner // width + i) for i in range(inner // width)], axis=0)
    return (
        undeal(back_out, 0),
        undeal(back_out, 1),
        undeal(back_grad, 1),
        undeal(back_grad, 0),
        vec_self[0],
        vec_self[1],
        block(packed_self, 0),
        block(packed_self, 1),
        block(packed_self, 2),
        block(packed_cross, 2),
        vec[7],
        vec[8],
        block(packed_cross, 1),
        block(packed_cross, 3),
        block(packed_cross, 4),
        block(packed_cross, 0),
        vec[0],
        vec[1],
        inner_grad,
        vec[3 : 3 + inner // width].reshape(-1),
        outer_grad,
        vec[2],
    )


def solution(mesh):
    split = P("rows", "seq", None)
    ids = P("rows", "seq")
    return jax.shard_map(
        local,
        mesh=mesh,
        in_specs=(split, split, split, ids, ids, split, split) + (P(),) * 18,
        out_specs=(split,) * 4 + (P(),) * 18,
        check_vma=False,
    )
```

```python
import functools
import math

import jax
import jax.numpy as jnp
from jax import lax
from jax.experimental import pallas as pl
from jax.experimental.pallas import tpu as pltpu
from jax.sharding import PartitionSpec as P

HEADS = 8
HEAD = 64
QUAD = 4 * HEAD
IDS = 5
epsilon = 1e-05
negative = -1e30
BOTH = ("rows", "seq")
bf16 = jnp.bfloat16
f32 = jnp.float32
LN2 = math.log(2.0)
QUERY_SCALE = HEAD ** (-0.5) / LN2
NN = ((1,), (0,))
NT = ((1,), (1,))
TN = ((0,), (0,))
GELU_A = math.sqrt(2.0 / math.pi)
GELU_B = 0.044715


def dot(left, right, dims):
    return lax.dot_general(left, right, (dims, ((), ())), preferred_element_type=f32)


def normalize(values):
    centered = values - jnp.mean(values, axis=-1, keepdims=True)
    scale = lax.rsqrt(jnp.mean(centered * centered, axis=-1, keepdims=True) + epsilon)
    return centered * scale, scale


def norm_back(normal, scale, gain, grad):
    inner = grad * gain
    mean = jnp.mean(inner, axis=-1, keepdims=True)
    along = jnp.mean(inner * normal, axis=-1, keepdims=True)
    return scale * (inner - mean - normal * along)


def mask_bias(row_ids, column_ids):
    rows = row_ids.shape[1]
    columns = column_ids.shape[1]
    spread = jnp.transpose(jnp.broadcast_to(row_ids.astype(f32), (128, rows)))
    spread = jnp.concatenate([spread] * (columns // 128), axis=1)
    return jnp.where(spread == column_ids.astype(f32), 0.0, negative)


def spread_ids(ids):
    spread = jnp.transpose(jnp.broadcast_to(ids.astype(f32), (128, ids.shape[1])))
    return jnp.concatenate([spread] * (QUAD // 128), axis=1)


def attend(q_ref, k_ref, v_ref, ids_q, ids_k, out_ref, lse_ref):
    count = q_ref.shape[0]
    length = k_ref.shape[0]
    group = lax.broadcasted_iota(jnp.int32, (count, QUAD), 1) // HEAD
    column = lax.broadcasted_iota(jnp.int32, (count, QUAD), 1) % HEAD
    group_k = lax.broadcasted_iota(jnp.int32, (length, QUAD), 1) // HEAD
    column_k = (lax.broadcasted_iota(jnp.int32, (length, QUAD), 1) % HEAD).astype(f32)
    slot = lax.broadcasted_iota(jnp.int32, (count, 128), 1)
    key_mask = jnp.where(column_k == spread_ids(ids_k), 1.0, 0.0).astype(bf16)
    seen = (column.astype(f32) == spread_ids(ids_q)) | (column >= IDS)
    query_mask = jnp.where(seen, 0.0, negative).astype(bf16)
    lse = jnp.zeros((count, 128), f32)
    for quad in range(HEADS // 4):
        span = slice(QUAD * quad, QUAD * quad + QUAD)
        queries = q_ref[:, span]
        keys = k_ref[:, span]
        values = v_ref[:, span]
        gathered = jnp.zeros((count, QUAD), f32)
        for head in range(4):
            beside = (head + 1) % 4
            own = jnp.where(group == head, queries, jnp.where(group == beside, query_mask, jnp.zeros_like(queries)))
            scores = dot(own, jnp.where(group_k == head, keys, key_mask), NT)
            top = jnp.max(scores, axis=1, keepdims=True)
            weights = jnp.exp2(scores - top).astype(bf16)
            result = dot(weights, jnp.where(group_k == head, values, jnp.ones_like(values)), NN)
            total = result[:, HEAD * beside : HEAD * beside + 1]
            gathered = jnp.where(group == head, result / total, gathered)
            lse = jnp.where(slot == 4 * quad + head, top + jnp.log2(total), lse)
        out_ref[:, span] = gathered.astype(bf16)
    lse_ref[...] = jnp.transpose(lse)[:HEADS]


def attend_back(q_ref, k_ref, v_ref, o_ref, lse_ref, bias_ref, do_ref, dqt_ref, take, base=0):
    count, columns = q_ref.shape
    lane = lax.broadcasted_iota(jnp.int32, (count, QUAD), 1) // HEAD
    product = do_ref[...].astype(f32) * o_ref[...].astype(f32)
    delta = jnp.sum(jnp.transpose(product).reshape(columns // HEAD, HEAD, count), axis=1)
    for quad in range(columns // QUAD):
        span = slice(QUAD * quad, QUAD * quad + QUAD)
        queries = q_ref[:, span]
        keys = k_ref[:, span]
        values = v_ref[:, span]
        grads = do_ref[:, span]
        keys_t = jnp.transpose(keys)
        key_grad = jnp.zeros((keys.shape[0], QUAD), f32)
        value_grad = jnp.zeros((keys.shape[0], QUAD), f32)
        for head in range(4):
            index = 4 * quad + head
            own_q = jnp.where(lane == head, queries, jnp.zeros_like(queries))
            own_g = jnp.where(lane == head, grads, jnp.zeros_like(grads))
            scores = dot(keys, own_q, NT) + bias_ref[...]
            probs = jnp.exp2(scores - lse_ref[base + index : base + index + 1, :])
            value_grad = value_grad + dot(probs.astype(bf16), own_g, NN)
            prob_grad = dot(values, own_g, NT)
            score_grad = (probs * (prob_grad - delta[index : index + 1, :])).astype(bf16)
            key_grad = key_grad + dot(score_grad, own_q, NN)
            rows = slice(HEAD * index, HEAD * index + HEAD)
            part = dot(keys_t[HEAD * head : HEAD * head + HEAD], score_grad, NN)
            dqt_ref[rows, :] = (part * HEAD ** (-0.5)).astype(bf16)
        take(span, key_grad * LN2, value_grad)


def self_forward(pieces, step, *refs):
    gain, shift, wq, wk, wv, wo, gain_two, shift_two, wcq = refs[pieces : pieces + 9]
    rest = refs[pieces + 9 :]
    if step == 0:
        n1, q, k, v, o, lse, mid, qc, ids, ids_m = rest
    else:
        ids, n1, q, k, v, o, lse, mid, qc = rest
    count = q.shape[0]
    group = count // 2
    xs = [ref.at[:group, :] for ref in refs[:pieces]]
    if step == 0:
        for index, ref in enumerate(refs[:pieces]):
            row = ref[group : group + 1, :].astype(f32)
            ids[:, index * group : (index + 1) * group] = row[:, :group]
            ids_m[:, index * group : (index + 1) * group] = row[:, group : 2 * group]
    for index, part in enumerate(xs):
        normal, _ = normalize(part[...].astype(f32))
        n1[index * group : (index + 1) * group, :] = (normal * gain[...] + shift[...]).astype(bf16)
    k[...] = dot(n1[...], wk[...], NN).astype(bf16)
    v[...] = dot(n1[...], wv[...], NN).astype(bf16)
    q[...] = (dot(n1[:count, :], wq[...], NN) * QUERY_SCALE).astype(bf16)
    attend(q, k, v, ids[:, :count], ids[...], o, lse)
    own = jnp.concatenate([part[...] for part in xs[: count // group]], axis=0).astype(f32)
    middle = own + dot(o[...], wo[...], NN)
    mid[...] = middle
    normal, _ = normalize(middle)
    low = (normal * gain_two[...] + shift_two[...]).astype(bf16)
    qc[...] = (dot(low, wcq[...], NN) * QUERY_SCALE).astype(bf16)


def memory_project(pieces, *refs):
    ms = refs[:pieces]
    wk, wv, k, v = refs[pieces:]
    group = ms[0].shape[0]
    for index, part in enumerate(ms):
        rows = slice(index * group, (index + 1) * group)
        k[rows, :] = dot(part[...], wk[...], NN).astype(bf16)
        v[rows, :] = dot(part[...], wv[...], NN).astype(bf16)


def cross_forward(ids_q, ids_k, q, k, v, mid, wo, o, lse, later):
    attend(q, k, v, ids_q[:, : q.shape[0]], ids_k[...], o, lse)
    later[...] = mid[...] + dot(o[...], wo[...], NN)


def part_out(core, keep, give, start, value):
    half, columns = value.shape[0] // 2, value.shape[1]
    value = value.astype(bf16)
    first = core[0] == 0
    keep[:, start : start + columns] = jnp.where(first, value[:half], value[half:])
    give[:, start : start + columns] = jnp.where(first, value[half:], value[:half])


def feed_forward(core, later_a, later_b, cot_a, cot_b, gain, shift, win, bin_, wout, bout, out_a, out_b, grad_a, grad_b, keep, give, vecs, cot, acc, dnorm):
    count = later_a.shape[0]
    width = later_a.shape[1]
    inner = win.shape[1]
    group = count // 2
    for step in range(2):
        for half, part in enumerate((cot_a, cot_b)):
            start = (2 * step + half) * group
            cot[start : start + group, :] = part[step * group : (step + 1) * group, :]
    later = jnp.concatenate([later_a[...], later_b[...]], axis=0)
    normal, scale = normalize(later)
    low = (normal * gain[...] + shift[...]).astype(bf16)
    bias_rows = []
    for index in range(inner // width):
        span = slice(index * width, (index + 1) * width)
        pre = dot(low, win[:, span], NN) + bin_[:, span]
        square = pre * pre
        tanh = jnp.tanh(GELU_A * (pre + GELU_B * (pre * square)))
        half = 0.5 * (1.0 + tanh)
        hidden = (pre * half).astype(bf16)
        slope = half + 0.5 * pre * (1.0 - tanh * tanh) * (GELU_A + (3.0 * GELU_A * GELU_B) * square)
        step = dot(hidden, wout[span, :], NN)
        hidden_grad = dot(cot[...], wout[span, :], NT)
        pre_grad = hidden_grad * slope
        pre_low = pre_grad.astype(bf16)
        bias_rows.append(jnp.sum(pre_grad, axis=0, keepdims=True))
        part_out(core, keep, give, index * width, dot(low, pre_low, TN))
        part_out(core, keep, give, inner + index * width, dot(hidden, cot[...], TN))
        back = dot(pre_low, win[:, span], NT)
        if index == 0:
            acc[...] = step
            dnorm[...] = back
        else:
            acc[...] = acc[...] + step
            dnorm[...] = dnorm[...] + back
    result = (later + acc[...] + bout[...]).astype(bf16)
    for half, out in enumerate((out_a, out_b)):
        for step in range(2):
            start = (2 * step + half) * group
            out[step * group : (step + 1) * group, :] = result[start : start + group]
    dn = dnorm[...]
    cots = cot[...].astype(f32)
    grad = cots + norm_back(normal, scale, gain[...], dn)
    grad_a[...] = grad[:count]
    grad_b[...] = grad[count:]
    rows = [
        jnp.sum(dn * normal, axis=0, keepdims=True),
        jnp.sum(dn, axis=0, keepdims=True),
        jnp.sum(cots, axis=0, keepdims=True),
    ] + bias_rows
    rows.append(jnp.zeros((16 - len(rows), width), f32))
    vecs[...] = jnp.concatenate(rows, axis=0)


def vector_block(rows):
    width = rows.shape[1]
    parts = [rows[:, 128 * block : 128 * block + 128] for block in range(width // 128)]
    return jnp.concatenate(parts + [jnp.zeros((width - 16 * (width // 128), 128), f32)], axis=0)


def cross_backward(pieces, others, *refs):
    last = pieces > 0
    grad, mid, oc, qc, lse, os_, k, v, ids_q, ids_k, wco, wcq, gain, shift, vecs_in = refs[pieces : pieces + 15]
    rest = refs[pieces + 15 :]
    if last:
        core, wck, wcv, sums_in, dk_in, dv_in, mg, keep, give, mem_own, mem_other, bias, do, dqt, dk, dv = rest
    else:
        mg, sums_out, dk, dv, vecs_out, bias, do, dqt = rest
    width = k.shape[1]
    count = qc.shape[0]
    bias[...] = mask_bias(ids_k[...], ids_q[:, :count])
    branch = grad[...].astype(bf16)
    do[...] = dot(branch, wco[...], NT).astype(bf16)

    def take(span, key_grad, value_grad):
        if last:
            key_grad = key_grad + dk_in[:, span].astype(f32)
            value_grad = value_grad + dv_in[:, span].astype(f32)
        dk[:, span] = key_grad.astype(bf16)
        dv[:, span] = value_grad.astype(bf16)

    attend_back(qc, k, v, oc, lse, bias, do, dqt, take)
    dq = jnp.transpose(dqt[...])
    normal, scale = normalize(mid[...])
    low = (normal * gain[...] + shift[...]).astype(bf16)
    dn = dot(dq, wcq[...], NT)
    middle_grad = grad[...] + norm_back(normal, scale, gain[...], dn)
    mg[...] = middle_grad
    sums = [dot(oc[...], branch, TN), dot(low, dq, TN), dot(os_[...], middle_grad.astype(bf16), TN)]
    gain_row = vecs_in[7:8, :] + jnp.sum(dn * normal, axis=0, keepdims=True)
    shift_row = vecs_in[8:9, :] + jnp.sum(dn, axis=0, keepdims=True)
    rows = jnp.concatenate([vecs_in[:7, :], gain_row, shift_row, vecs_in[9:, :]], axis=0)
    if not last:
        vecs_out[...] = rows
        for index, value in enumerate(sums):
            sums_out[:, index * width : (index + 1) * width] = value.astype(bf16)
        return
    grad_k = 0.0
    grad_v = 0.0
    group = refs[0].shape[0]
    for index, part in enumerate(refs[:pieces]):
        span = slice(index * group, (index + 1) * group)
        grad_k = grad_k + dot(part[...], dk[span, :], TN)
        grad_v = grad_v + dot(part[...], dv[span, :], TN)
    for index, value in enumerate(sums):
        part_out(core, keep, give, index * width, value + sums_in[:, index * width : (index + 1) * width].astype(f32))
    part_out(core, keep, give, 3 * width, grad_k)
    part_out(core, keep, give, 4 * width, grad_v)
    part_out(core, keep, give, 5 * width, vector_block(rows))
    mem_own[...] = dot(dk[:count, :], wck[...], NT) + dot(dv[:count, :], wcv[...], NT)
    if others:
        mem_other[...] = (dot(dk[count:, :], wck[...], NT) + dot(dv[count:, :], wcv[...], NT)).astype(bf16)


def self_backward(step, quad, *refs):
    mg, wo, o, q, k, v, lse, ids, n1, wq, wk, wv, gain, shift = refs[:14]
    rest = list(refs[14:])
    bias, do, dqt, dk, dv = rest[-5:]
    rest = rest[:-5]
    count, columns = q.shape
    bias[...] = mask_bias(ids[...], ids[:, :count])
    do[...] = dot(mg[...].astype(bf16), wo[...], NT).astype(bf16)

    def take(span, key_grad, value_grad):
        dk[:, span] = key_grad.astype(bf16)
        dv[:, span] = value_grad.astype(bf16)

    attend_back(q, k, v, o, lse, bias, do, dqt, take, 4 * quad)
    dq = jnp.transpose(dqt[...])
    low = n1[...]
    acts = (low[:count], low, low)
    grads = (dq, dk[...], dv[...])
    sums = [dot(act, value, TN) for act, value in zip(acts, grads)]
    gain_term = 0.0
    shift_term = 0.0
    for value, grad, weight in zip(sums, grads, (wq, wk, wv)):
        weight = weight[...].astype(f32)
        column = jnp.sum(grad.astype(f32), axis=0, keepdims=True)
        gain_term = gain_term + jnp.sum(weight * (value - shift[...] * column), axis=1, keepdims=True)
        shift_term = shift_term + jnp.sum(weight * column, axis=1, keepdims=True)
    lane = lax.broadcasted_iota(jnp.int32, (low.shape[1], 128), 1)
    vec = jnp.where(lane == 0, gain_term / gain[...], jnp.where(lane == 1, shift_term, 0.0))
    if step or quad:
        vec = vec + rest.pop(0)[...]
    if step:
        before = rest.pop(0)
        sums = [value + before[:, i * columns : (i + 1) * columns].astype(f32) for i, value in enumerate(sums)]
    if step and quad:
        core, first, keep, give = rest
        for index, value in enumerate(sums):
            earlier = first[:, index * columns : (index + 1) * columns].astype(f32)
            part_out(core, keep, give, 2 * index * columns, earlier)
            part_out(core, keep, give, (2 * index + 1) * columns, value)
        part_out(core, keep, give, 6 * columns, vec)
        return
    if not step:
        own = dot(dk[:count, :], wk[...], NT) + dot(dv[:count, :], wv[...], NT) + dot(dq, wq[...], NT)
        more = dk.shape[0] > count
        other = dot(dk[count:, :], wk[...], NT) + dot(dv[count:, :], wv[...], NT) if more else None
        if quad:
            own = own + rest.pop(0)[...]
            before = rest.pop(0)
            other = other + before[...].astype(f32) if more else None
        ng_own, ng_other = rest[-2:]
        ng_own[...] = own
        if more:
            ng_other[...] = other.astype(bf16)
    sums_out, vec_out = rest[:2]
    vec_out[...] = vec
    for index, value in enumerate(sums):
        sums_out[:, index * columns : (index + 1) * columns] = value.astype(bf16)


def input_backward(parts, xa, xb, mg, ng, gain, *refs):
    received = refs[:parts]
    halves = refs[parts:]
    count = mg.shape[0]
    group = count // 2
    grad = ng[...]
    for part in received:
        grad = grad + part[...].astype(f32)
    x = jnp.concatenate([xa[:group, :], xb[:group, :]], axis=0).astype(f32)
    normal, scale = normalize(x)
    result = (mg[...] + norm_back(normal, scale, gain[...], grad)).astype(bf16)
    for half, out in enumerate(halves):
        out[...] = result[half * group : (half + 1) * group]


def call(body, outs, args, scratch=(), flops=0, name=None, blocks=None):
    moved = sum(math.prod(a.shape) * a.dtype.itemsize for a in args)
    moved += sum(math.prod(s) * jnp.dtype(d).itemsize for s, d in outs)
    blocks = blocks or {}

    def spec(index, value):
        if value.dtype == jnp.int32:
            return pl.BlockSpec(memory_space=pltpu.SMEM)
        if index in blocks:
            shape, place = blocks[index]
            return pl.BlockSpec(shape, lambda i: place)
        return pl.BlockSpec(value.shape, lambda i: (0,) * value.ndim)

    return pl.pallas_call(
        body,
        grid=(1,),
        in_specs=[spec(index, value) for index, value in enumerate(args)],
        out_specs=[pl.BlockSpec(s, lambda i, n=len(s): (0,) * n) for s, d in outs],
        out_shape=[jax.ShapeDtypeStruct(s, d) for s, d in outs],
        scratch_shapes=[pltpu.VMEM(s, d) for s, d in scratch],
        compiler_params=pltpu.CompilerParams(vmem_limit_bytes=58 * 2**20),
        cost_estimate=pl.CostEstimate(flops=int(flops), bytes_accessed=int(moved) if flops > 1 else 1, transcendentals=0),
        name=name,
    )(*args)


def local(
    inputs_one,
    inputs_two,
    memory,
    target_ids,
    memory_ids,
    cotangent_one,
    cotangent_two,
    first_gain,
    first_bias,
    self_query,
    self_key,
    self_value,
    self_output,
    second_gain,
    second_bias,
    cross_query,
    cross_key,
    cross_value,
    cross_output,
    third_gain,
    third_bias,
    inner_weight,
    inner_bias,
    outer_weight,
    outer_bias,
):
    ring = lax.axis_size("seq")
    pairs = lax.axis_size("rows") // 2
    place = lax.axis_index("seq")
    held = inputs_one.shape[0]
    group = inputs_one.shape[1]
    width = inputs_one.shape[2]
    inner = inner_weight.shape[1]
    workers = ring // held
    count = 2 * group
    length = workers * count
    pieces = 2 * workers
    others = workers - 1
    odd = place % 2

    def flat(pair, member):
        return (2 * pair + member % 2) * ring + member // 2

    def dealt(swap):
        links = []
        for pair in range(pairs):
            for core in range(2):
                for spot in range(ring):
                    row = held * core + (spot + swap) % 2
                    links.append((flat(pair, 2 * spot + core), flat(pair, row * workers + spot // 2)))
        return links

    def turned(shift):
        links = []
        for pair in range(pairs):
            for member in range(2 * ring):
                row, worker = divmod(member, workers)
                links.append((flat(pair, row * workers + (worker + shift) % workers), flat(pair, member)))
        return links

    def reverse(links):
        return [(b, a) for a, b in links]

    def send(value, links):
        return lax.ppermute(value, BOTH, links)

    def pick(value, swap):
        return lax.dynamic_index_in_dim(value, odd if swap == 0 else 1 - odd, 0, keepdims=False)

    def deal(*values):
        return [send(jnp.concatenate([pick(v, s) for v in values], axis=0), dealt(s)) for s in range(2)]

    def row_of(parts):
        whole = list(parts)
        for shift in range(1, workers):
            whole += [send(part, turned(shift)) for part in parts]
        return whole

    def back_sum(rest):
        return [
            send(rest[(shift - 1) * count : shift * count], reverse(turned(shift))) for shift in range(1, workers)
        ]

    def row(vector):
        return vector.reshape(1, -1)

    def give_back(halves):
        return [send(half, reverse(dealt(s))) for s, half in enumerate(halves)]

    def undeal(parts, step):
        parts = [part[step * group : (step + 1) * group] for part in parts]
        return jnp.where(odd == 0, jnp.stack(parts), jnp.stack(parts[::-1]))

    spot = lax.axis_index("rows")
    core = spot % 2
    bits = pairs.bit_length() - 1

    def chip_stage(turn):
        links = []
        for i in range(2 * pairs):
            links.append((i, i ^ (2 << ((turn + i % 2) % bits))))
        bit = jnp.where(core == 0, (spot >> (1 + turn % bits)) & 1, (spot >> (1 + (turn + 1) % bits)) & 1)
        return bit, links

    stages = [(core, [(i, i ^ 1) for i in range(2 * pairs)])] + [chip_stage(turn) for turn in range(bits)]

    def split(parts, stage):
        bit, links = stages[stage]
        half = parts[0].shape[0] // 2
        parts = [part.reshape((2, half) + part.shape[1:]) for part in parts]
        take = lambda i: total(*[lax.dynamic_index_in_dim(part, i, 0, keepdims=False) for part in parts])
        return take(bit), lax.ppermute(take(1 - bit), "rows", links)

    def total(first, *rest):
        result = first.astype(f32)
        for part in rest:
            result = result + part.astype(f32)
        return result.astype(bf16)

    def join_sends(value, stage):
        return [value, lax.ppermute(value, "rows", stages[stage][1])]

    def joined(parts, stage):
        value, other = parts
        bit = stages[stage][0]
        return jnp.where(bit == 0, jnp.concatenate([value, other]), jnp.concatenate([other, value]))

    def join(value, stage):
        return joined(join_sends(value, stage), stage)

    turns = ring.bit_length() - 1

    def along(value, turn):
        return [value, lax.ppermute(value, "seq", [(i, i ^ (1 << turn)) for i in range(ring)])]

    direct = {
        "core": ("rows", 2, core, [[(i, i ^ 1) for i in range(2 * pairs)]]),
        "chips": ("rows", pairs, spot // 2, [[(i, i ^ (2 * k)) for i in range(2 * pairs)] for k in range(1, pairs)]),
        "line": ("seq", ring, place, [[(i, i ^ k) for i in range(ring)] for k in range(1, ring)]),
    }

    def swap(keep, give):
        return [keep, lax.ppermute(give, "rows", stages[0][1])]

    def spread(parts, stage):
        axis, size, index, links = direct[stage]
        share = parts[0].shape[0] // size
        parts = [part.reshape((size, share) + part.shape[1:]) for part in parts]
        take = lambda i: total(*[lax.dynamic_index_in_dim(part, i, 0, keepdims=False) for part in parts])
        return [take(index)] + [lax.ppermute(take(index ^ (k + 1)), axis, link) for k, link in enumerate(links)]

    def gather_sends(value, stage):
        axis, size, index, links = direct[stage]
        return [value] + [lax.ppermute(value, axis, link) for link in links]

    def gathered(parts, stage):
        index = direct[stage][2]
        size = len(parts)
        levels = size.bit_length() - 1
        result = jnp.stack(parts).reshape((2,) * levels + parts[0].shape)
        for level in range(levels):
            result = jnp.where((index >> level) & 1 == 1, jnp.flip(result, levels - 1 - level), result)
        return result.reshape((size * parts[0].shape[0],) + parts[0].shape[1:])

    def gather(value, stage):
        return gathered(gather_sends(value, stage), stage)

    def after(values, *needed):
        return lax.optimization_barrier((values, needed))[0]

    g1, b1, g2, b2, g3, b3 = map(
        row, (first_gain, first_bias, second_gain, second_bias, third_gain, third_bias)
    )
    id_block = jnp.concatenate([target_ids, memory_ids], axis=1).astype(bf16)[:, None, :]
    id_block = jnp.pad(id_block, ((0, 0), (0, 15), (0, width - 2 * group)))
    own = deal(inputs_one, id_block)
    xs = row_of(own)
    own_memory = deal(after(memory, *xs))

    tokens = (count, width)
    whole = (length, width)
    lse = (HEADS, count)
    scores = 2 * count * length * width
    square = 2 * count * width * width

    def run_self(xs, step, *ids):
        rows = [((1, length), f32)] * 2 if step == 0 else []
        return call(
            functools.partial(self_forward, pieces, step),
            [
                (whole, bf16), (tokens, bf16), (whole, bf16), (whole, bf16), (tokens, bf16), (lse, f32), (tokens, f32),
                (tokens, bf16), *rows,
            ],
            [*xs, g1, b1, self_query, self_key, self_value, self_output, g2, b2, cross_query, *ids],
            [],
            8 * scores + (3 + 2 * workers) * square,
            "self_forward",
        )

    def run_cross(qc, mid):
        return call(
            cross_forward,
            [(tokens, bf16), (lse, f32), (tokens, f32)],
            [ids_t, ids_m, qc, mem_k, mem_v, mid, cross_output],
            [],
            8 * scores + square,
            "cross_forward",
        )

    n1_a, q_a, k_a, v_a, o_a, lse_a, mid_a, qc_a, ids_t, ids_m = run_self(xs, 0)
    mem = row_of(after(own_memory, qc_a))
    own_two = deal(after(inputs_two, *mem))
    mem_k, mem_v = call(
        functools.partial(memory_project, pieces),
        [(whole, bf16), (whole, bf16)],
        [*mem, cross_key, cross_value],
        flops=2 * workers * square,
        name="memory_project",
    )
    oc_a, lsec_a, later_a = run_cross(qc_a, mid_a)
    xs_two = row_of(after(own_two, later_a))
    cots = deal(*after((cotangent_one, cotangent_two), *xs_two))
    n1_b, q_b, k_b, v_b, o_b, lse_b, mid_b, qc_b = run_self(xs_two, 1, ids_t)
    oc_b, lsec_b, later_b = run_cross(qc_b, mid_b)
    both = (2 * count, width)
    half = width // 2
    which = jnp.reshape(core, (1,)).astype(jnp.int32)
    out_a, out_b, lg_a, lg_b, keep, give, vecs = call(
        feed_forward,
        [
            ((2 * group, width), bf16), ((2 * group, width), bf16), (tokens, f32), (tokens, f32),
            ((half, 2 * inner), bf16), ((half, 2 * inner), bf16), ((16, width), f32),
        ],
        [which, later_a, later_b, *cots, g3, b3, inner_weight, row(inner_bias), outer_weight, row(outer_bias)],
        [(both, bf16), (both, f32), (both, f32)],
        2 * 6 * square * inner // width,
        "feed_forward",
    )
    rest = (max(others, 1) * count, width)
    back_scratch = [((length, count), f32), (tokens, bf16), ((width, count), bf16)]
    ff_parts = swap(keep, give)
    back_out = give_back([out_a, out_b])
    mg_a, cross_sums, dk_a, dv_a, vecs = call(
        functools.partial(cross_backward, 0, others),
        [(tokens, f32), ((width, 3 * width), bf16), (whole, bf16), (whole, bf16), ((16, width), f32)],
        [lg_a, mid_a, oc_a, qc_a, lsec_a, o_a, mem_k, mem_v, ids_t, ids_m, cross_output, cross_query, g2, b2, vecs],
        back_scratch,
        20 * scores + 5 * square,
        "cross_backward",
    )
    lg_b = after(lg_b, mg_a, *ff_parts, *back_out)
    ff_parts = split(after(ff_parts, mg_a), 1)
    mg_b, keep, give, mem_own, mem_other = call(
        functools.partial(cross_backward, pieces, others),
        [(tokens, f32), ((half, 5 * width + 128), bf16), ((half, 5 * width + 128), bf16), (tokens, f32), (rest, bf16)],
        [
            *mem, lg_b, mid_b, oc_b, qc_b, lsec_b, o_b, mem_k, mem_v, ids_t, ids_m, cross_output, cross_query,
            g2, b2, vecs, which, cross_key, cross_value, cross_sums, dk_a, dv_a,
        ],
        back_scratch + [(whole, bf16), (whole, bf16)],
        20 * scores + 14 * square,
        "cross_backward_last",
    )

    def run_back(step, quad, mg, extra, outs):
        o, q, k, v, norm, lse = ((o_a, q_a, k_a, v_a, n1_a, lse_a), (o_b, q_b, k_b, v_b, n1_b, lse_b))[step]
        columns = (0, quad)
        blocks = {1: ((QUAD, width), (quad, 0))}
        blocks.update({i: ((count, QUAD), columns) for i in (2, 3)})
        blocks.update({i: ((length, QUAD), columns) for i in (4, 5)})
        blocks.update({i: ((width, QUAD), columns) for i in (9, 10, 11)})
        return call(
            functools.partial(self_backward, step, quad),
            outs,
            [
                mg, self_output, o, q, k, v, lse, ids_t, norm, self_query, self_key, self_value,
                first_gain.reshape(-1, 1), first_bias.reshape(-1, 1), *extra,
            ],
            [
                ((length, count), f32), ((count, QUAD), bf16), ((QUAD, count), bf16),
                ((length, QUAD), bf16), ((length, QUAD), bf16),
            ],
            10 * scores,
            "self_backward",
            blocks,
        )

    sums_shape = ((width, 3 * QUAD), bf16)
    vec_shape = ((width, 128), f32)
    keep_shape = ((half, 3 * width + 128), bf16)
    mg_a = after(mg_a, mg_b, *ff_parts)
    ff_parts = split(after(ff_parts, mg_b), 2)
    for turn in range(2, bits):
        ff_parts = split(ff_parts, 1 + turn)
    cross_parts = swap(keep, give)
    memory_parts = back_sum(mem_other)
    sums_0, vec, ng_own, ng_other = run_back(0, 0, mg_a, [], [sums_shape, vec_shape, (tokens, f32), (rest, bf16)])
    mg_a = after(mg_a, vec, *ff_parts, *cross_parts, *memory_parts)
    ff_parts = spread(after(ff_parts, vec), "line")
    cross_parts = split(after(cross_parts, vec), 1)
    sums_1, vec, ng_own, ng_other = run_back(
        0, 1, mg_a, [vec, ng_own, ng_other], [sums_shape, vec_shape, (tokens, f32), (rest, bf16)]
    )
    mg_b = after(mg_b, vec, *cross_parts, *ff_parts)
    ff_parts = gather_sends(total(*after(ff_parts, vec)), "line")
    cross_parts = split(after(cross_parts, vec), 2)
    sums_0, vec = run_back(1, 0, mg_b, [vec, sums_0], [sums_shape, vec_shape])
    mg_b = after(mg_b, vec, *cross_parts, *ff_parts)
    ready = (*cross_parts, *ff_parts)
    ff_sum = gathered(after(ff_parts, vec), "line")
    for stage in reversed(range(3, 1 + bits)):
        ff_sum = join(ff_sum, stage)
    ff_parts = join_sends(ff_sum, 2)
    received = back_sum(after(ng_other, vec, *ready))
    memory_sum = after(mem_own, vec, *ready)
    for part in memory_parts:
        memory_sum = memory_sum + part.astype(f32)
    memory_sum = memory_sum.astype(bf16)
    back_memory = give_back([memory_sum[:group], memory_sum[group:]])
    cross_parts = after(cross_parts, vec)
    for turn in range(2, bits):
        cross_parts = split(cross_parts, 1 + turn)
    cross_parts = along(total(*cross_parts), 0)
    keep, give = run_back(1, 1, mg_b, [vec, sums_1, which, sums_0], [keep_shape, keep_shape])
    keep, give = after((keep, give), *ff_parts, *cross_parts, *received, *back_memory)
    self_parts = swap(keep, give)
    ff_parts = join_sends(joined(after(ff_parts, keep), 2), 1)
    cross_parts = along(total(*after(cross_parts, keep)), 1)
    for turn in range(2, turns):
        cross_parts = along(total(*cross_parts), turn)
    halves = call(
        functools.partial(input_backward, others),
        [((group, width), bf16), ((group, width), bf16)],
        [*own, mg_a, after(ng_own, keep), g1, *received],
        name="input_backward",
    )
    self_parts = spread(after(self_parts, *halves), "chips")
    both_parts = lax.optimization_barrier((self_parts, cross_parts, ff_parts))
    self_parts = spread(both_parts[0], "line")
    cross_parts = join_sends(total(*both_parts[1]), bits)
    both_parts = lax.optimization_barrier((self_parts, cross_parts, both_parts[2]))
    self_parts = gather_sends(total(*both_parts[0]), "line")
    cross_sum = joined(both_parts[1], bits)
    for stage in reversed(range(2, bits)):
        cross_sum = join(cross_sum, stage)
    cross_parts = join_sends(cross_sum, 1)
    ff_parts = join_sends(joined(after(both_parts[2], self_parts[0]), 1), 0)
    both_parts = lax.optimization_barrier((self_parts, cross_parts))
    self_parts = gather_sends(gathered(both_parts[0], "line"), "chips")
    cross_parts = join_sends(joined(both_parts[1], 1), 0)
    back_input = give_back(after(halves, *both_parts[0]))
    ff_parts = after(ff_parts, *both_parts[0])

    def block(parts, index):
        return joined([part[:, index * width : (index + 1) * width] for part in parts], 0).astype(f32)

    def vectors(packed, start):
        rows = packed[: 16 * (width // 128), start : start + 128].astype(f32)
        return jnp.swapaxes(rows.reshape(width // 128, 16, 128), 0, 1).reshape(16, width)

    cross_blocks = [block(cross_parts, index) for index in range(5)]
    inner_grad = joined([part[:, :inner] for part in ff_parts], 0).astype(f32)
    outer_grad = jnp.concatenate([block(ff_parts, inner // width + i) for i in range(inner // width)], axis=0)
    self_parts, cross_blocks, inner_grad, outer_grad, back_input = lax.optimization_barrier(
        (self_parts, cross_blocks, inner_grad, outer_grad, back_input)
    )
    self_parts = join_sends(gathered(self_parts, "chips"), 0)

    vec = vectors(joined([part[:, 5 * width :] for part in cross_parts], 0), 0)
    vec_self = joined([part[:, 3 * width : 3 * width + 2] for part in self_parts], 0).astype(f32)
    return (
        undeal(back_out, 0),
        undeal(back_out, 1),
        undeal(back_input, 0),
        undeal(back_memory, 0),
        vec_self[:, 0],
        vec_self[:, 1],
        block(self_parts, 0),
        block(self_parts, 1),
        block(self_parts, 2),
        cross_blocks[2],
        vec[7],
        vec[8],
        cross_blocks[1],
        cross_blocks[3],
        cross_blocks[4],
        cross_blocks[0],
        vec[0],
        vec[1],
        inner_grad,
        vec[3 : 3 + inner // width].reshape(-1),
        outer_grad,
        vec[2],
    )


def solution(mesh):
    split = P("rows", "seq", None)
    ids = P("rows", "seq")
    return jax.shard_map(
        local,
        mesh=mesh,
        in_specs=(split, split, split, ids, ids, split, split) + (P(),) * 18,
        out_specs=(split,) * 4 + (P(),) * 18,
        check_vma=False,
    )
```

```python
import functools
import math

import jax
import jax.numpy as jnp
from jax import lax
from jax.experimental import pallas as pl
from jax.experimental.pallas import tpu as pltpu
from jax.sharding import PartitionSpec as P

HEADS = 8
HEAD = 64
QUAD = 4 * HEAD
IDS = 5
VMEM_MIB = 26
epsilon = 1e-05
negative = -1e30
BOTH = ("rows", "seq")
bf16 = jnp.bfloat16
f32 = jnp.float32
LN2 = math.log(2.0)
QUERY_SCALE = HEAD ** (-0.5) / LN2
NN = ((1,), (0,))
NT = ((1,), (1,))
TN = ((0,), (0,))
GELU_A = math.sqrt(2.0 / math.pi)
GELU_B = 0.044715


def dot(left, right, dims):
    return lax.dot_general(left, right, (dims, ((), ())), preferred_element_type=f32)


def normalize(values):
    centered = values - jnp.mean(values, axis=-1, keepdims=True)
    scale = lax.rsqrt(jnp.mean(centered * centered, axis=-1, keepdims=True) + epsilon)
    return centered * scale, scale


def norm_back(normal, scale, gain, grad):
    inner = grad * gain
    mean = jnp.mean(inner, axis=-1, keepdims=True)
    along = jnp.mean(inner * normal, axis=-1, keepdims=True)
    return scale * (inner - mean - normal * along)


def mask_bias(row_ids, column_ids):
    rows = row_ids.shape[1]
    columns = column_ids.shape[1]
    spread = jnp.transpose(jnp.broadcast_to(row_ids.astype(f32), (128, rows)))
    spread = jnp.concatenate([spread] * (columns // 128), axis=1)
    return jnp.where(spread == column_ids.astype(f32), 0.0, negative)


def spread_ids(ids):
    spread = jnp.transpose(jnp.broadcast_to(ids.astype(f32), (128, ids.shape[1])))
    return jnp.concatenate([spread] * (QUAD // 128), axis=1)


def attend(q_ref, k_ref, v_ref, ids_q, ids_k, out_ref, lse_ref):
    count = q_ref.shape[0]
    length = k_ref.shape[0]
    group = lax.broadcasted_iota(jnp.int32, (count, QUAD), 1) // HEAD
    column = lax.broadcasted_iota(jnp.int32, (count, QUAD), 1) % HEAD
    group_k = lax.broadcasted_iota(jnp.int32, (length, QUAD), 1) // HEAD
    column_k = (lax.broadcasted_iota(jnp.int32, (length, QUAD), 1) % HEAD).astype(f32)
    slot = lax.broadcasted_iota(jnp.int32, (count, 128), 1)
    key_mask = jnp.where(column_k == spread_ids(ids_k), 1.0, 0.0).astype(bf16)
    seen = (column.astype(f32) == spread_ids(ids_q)) | (column >= IDS)
    query_mask = jnp.where(seen, 0.0, negative).astype(bf16)
    lse = jnp.zeros((count, 128), f32)
    for quad in range(HEADS // 4):
        span = slice(QUAD * quad, QUAD * quad + QUAD)
        queries = q_ref[:, span]
        keys = k_ref[:, span]
        values = v_ref[:, span]
        gathered = jnp.zeros((count, QUAD), f32)
        for head in range(4):
            beside = (head + 1) % 4
            own = jnp.where(group == head, queries, jnp.where(group == beside, query_mask, jnp.zeros_like(queries)))
            scores = dot(own, jnp.where(group_k == head, keys, key_mask), NT)
            top = jnp.max(scores, axis=1, keepdims=True)
            weights = jnp.exp2(scores - top).astype(bf16)
            result = dot(weights, jnp.where(group_k == head, values, jnp.ones_like(values)), NN)
            total = result[:, HEAD * beside : HEAD * beside + 1]
            gathered = jnp.where(group == head, result / total, gathered)
            lse = jnp.where(slot == 4 * quad + head, top + jnp.log2(total), lse)
        out_ref[:, span] = gathered.astype(bf16)
    lse_ref[...] = jnp.transpose(lse)[:HEADS]


def attend_back(q_ref, k_ref, v_ref, o_ref, lse_ref, bias_ref, do_ref, dqt_ref, take, base=0):
    count, columns = q_ref.shape
    lane = lax.broadcasted_iota(jnp.int32, (count, QUAD), 1) // HEAD
    product = do_ref[...].astype(f32) * o_ref[...].astype(f32)
    delta = jnp.sum(jnp.transpose(product).reshape(columns // HEAD, HEAD, count), axis=1)
    for quad in range(columns // QUAD):
        span = slice(QUAD * quad, QUAD * quad + QUAD)
        queries = q_ref[:, span]
        keys = k_ref[:, span]
        values = v_ref[:, span]
        grads = do_ref[:, span]
        keys_t = jnp.transpose(keys)
        key_grad = jnp.zeros((keys.shape[0], QUAD), f32)
        value_grad = jnp.zeros((keys.shape[0], QUAD), f32)
        for head in range(4):
            index = 4 * quad + head
            own_q = jnp.where(lane == head, queries, jnp.zeros_like(queries))
            own_g = jnp.where(lane == head, grads, jnp.zeros_like(grads))
            scores = dot(keys, own_q, NT) + bias_ref[...]
            probs = jnp.exp2(scores - lse_ref[base + index : base + index + 1, :])
            value_grad = value_grad + dot(probs.astype(bf16), own_g, NN)
            prob_grad = dot(values, own_g, NT)
            score_grad = (probs * (prob_grad - delta[index : index + 1, :])).astype(bf16)
            key_grad = key_grad + dot(score_grad, own_q, NN)
            rows = slice(HEAD * index, HEAD * index + HEAD)
            part = dot(keys_t[HEAD * head : HEAD * head + HEAD], score_grad, NN)
            dqt_ref[rows, :] = (part * HEAD ** (-0.5)).astype(bf16)
        take(span, key_grad * LN2, value_grad)


def self_forward(pieces, step, *refs):
    gain, shift, wq, wk, wv, wo, gain_two, shift_two, wcq = refs[pieces : pieces + 9]
    rest = refs[pieces + 9 :]
    if step == 0:
        n1, q, k, v, o, lse, mid, qc, ids, ids_m = rest
    else:
        ids, n1, q, k, v, o, lse, mid, qc = rest
    count = q.shape[0]
    group = count // 2
    xs = [ref.at[:group, :] for ref in refs[:pieces]]
    if step == 0:
        for index, ref in enumerate(refs[:pieces]):
            row = ref[group : group + 1, :].astype(f32)
            ids[:, index * group : (index + 1) * group] = row[:, :group]
            ids_m[:, index * group : (index + 1) * group] = row[:, group : 2 * group]
    for index, part in enumerate(xs):
        normal, _ = normalize(part[...].astype(f32))
        n1[index * group : (index + 1) * group, :] = (normal * gain[...] + shift[...]).astype(bf16)
    k[...] = dot(n1[...], wk[...], NN).astype(bf16)
    v[...] = dot(n1[...], wv[...], NN).astype(bf16)
    q[...] = (dot(n1[:count, :], wq[...], NN) * QUERY_SCALE).astype(bf16)
    attend(q, k, v, ids[:, :count], ids[...], o, lse)
    own = jnp.concatenate([part[...] for part in xs[: count // group]], axis=0).astype(f32)
    middle = own + dot(o[...], wo[...], NN)
    mid[...] = middle
    normal, _ = normalize(middle)
    low = (normal * gain_two[...] + shift_two[...]).astype(bf16)
    qc[...] = (dot(low, wcq[...], NN) * QUERY_SCALE).astype(bf16)


def memory_project(pieces, *refs):
    ms = refs[:pieces]
    wk, wv, k, v = refs[pieces:]
    group = ms[0].shape[0]
    for index, part in enumerate(ms):
        rows = slice(index * group, (index + 1) * group)
        k[rows, :] = dot(part[...], wk[...], NN).astype(bf16)
        v[rows, :] = dot(part[...], wv[...], NN).astype(bf16)


def cross_forward(ids_q, ids_k, q, k, v, mid, wo, o, lse, later):
    attend(q, k, v, ids_q[:, : q.shape[0]], ids_k[...], o, lse)
    later[...] = mid[...] + dot(o[...], wo[...], NN)


def part_out(core, keep, give, start, value):
    half, columns = value.shape[0] // 2, value.shape[1]
    value = value.astype(bf16)
    first = core[0] == 0
    keep[:, start : start + columns] = jnp.where(first, value[:half], value[half:])
    give[:, start : start + columns] = jnp.where(first, value[half:], value[:half])


def feed_forward(core, later_a, later_b, cot_a, cot_b, gain, shift, win, bin_, wout, bout, out_a, out_b, grad_a, grad_b, keep, give, vecs, cot, acc, dnorm):
    count = later_a.shape[0]
    width = later_a.shape[1]
    inner = win.shape[1]
    group = count // 2
    for step in range(2):
        for half, part in enumerate((cot_a, cot_b)):
            start = (2 * step + half) * group
            cot[start : start + group, :] = part[step * group : (step + 1) * group, :]
    later = jnp.concatenate([later_a[...], later_b[...]], axis=0)
    normal, scale = normalize(later)
    low = (normal * gain[...] + shift[...]).astype(bf16)
    bias_rows = []
    for index in range(inner // width):
        span = slice(index * width, (index + 1) * width)
        pre = dot(low, win[:, span], NN) + bin_[:, span]
        square = pre * pre
        tanh = jnp.tanh(GELU_A * (pre + GELU_B * (pre * square)))
        half = 0.5 * (1.0 + tanh)
        hidden = (pre * half).astype(bf16)
        slope = half + 0.5 * pre * (1.0 - tanh * tanh) * (GELU_A + (3.0 * GELU_A * GELU_B) * square)
        step = dot(hidden, wout[span, :], NN)
        hidden_grad = dot(cot[...], wout[span, :], NT)
        pre_grad = hidden_grad * slope
        pre_low = pre_grad.astype(bf16)
        bias_rows.append(jnp.sum(pre_grad, axis=0, keepdims=True))
        part_out(core, keep, give, index * width, dot(low, pre_low, TN))
        part_out(core, keep, give, inner + index * width, dot(hidden, cot[...], TN))
        back = dot(pre_low, win[:, span], NT)
        if index == 0:
            acc[...] = step
            dnorm[...] = back
        else:
            acc[...] = acc[...] + step
            dnorm[...] = dnorm[...] + back
    result = (later + acc[...] + bout[...]).astype(bf16)
    for half, out in enumerate((out_a, out_b)):
        for step in range(2):
            start = (2 * step + half) * group
            out[step * group : (step + 1) * group, :] = result[start : start + group]
    dn = dnorm[...]
    cots = cot[...].astype(f32)
    grad = cots + norm_back(normal, scale, gain[...], dn)
    grad_a[...] = grad[:count]
    grad_b[...] = grad[count:]
    rows = [
        jnp.sum(dn * normal, axis=0, keepdims=True),
        jnp.sum(dn, axis=0, keepdims=True),
        jnp.sum(cots, axis=0, keepdims=True),
    ] + bias_rows
    rows.append(jnp.zeros((16 - len(rows), width), f32))
    vecs[...] = jnp.concatenate(rows, axis=0)


def vector_block(rows):
    width = rows.shape[1]
    parts = [rows[:, 128 * block : 128 * block + 128] for block in range(width // 128)]
    return jnp.concatenate(parts + [jnp.zeros((width - 16 * (width // 128), 128), f32)], axis=0)


def cross_backward(pieces, others, *refs):
    last = pieces > 0
    grad, mid, oc, qc, lse, os_, k, v, ids_q, ids_k, wco, wcq, gain, shift, vecs_in = refs[pieces : pieces + 15]
    rest = refs[pieces + 15 :]
    if last:
        core, wck, wcv, sums_in, dk_in, dv_in, mg, keep, give, mem_own, mem_other, bias, do, dqt, dk, dv = rest
    else:
        mg, sums_out, dk, dv, vecs_out, bias, do, dqt = rest
    width = k.shape[1]
    count = qc.shape[0]
    bias[...] = mask_bias(ids_k[...], ids_q[:, :count])
    branch = grad[...].astype(bf16)
    do[...] = dot(branch, wco[...], NT).astype(bf16)

    def take(span, key_grad, value_grad):
        if last:
            key_grad = key_grad + dk_in[:, span].astype(f32)
            value_grad = value_grad + dv_in[:, span].astype(f32)
        dk[:, span] = key_grad.astype(bf16)
        dv[:, span] = value_grad.astype(bf16)

    attend_back(qc, k, v, oc, lse, bias, do, dqt, take)
    dq = jnp.transpose(dqt[...])
    normal, scale = normalize(mid[...])
    low = (normal * gain[...] + shift[...]).astype(bf16)
    dn = dot(dq, wcq[...], NT)
    middle_grad = grad[...] + norm_back(normal, scale, gain[...], dn)
    mg[...] = middle_grad
    sums = [dot(oc[...], branch, TN), dot(low, dq, TN), dot(os_[...], middle_grad.astype(bf16), TN)]
    gain_row = vecs_in[7:8, :] + jnp.sum(dn * normal, axis=0, keepdims=True)
    shift_row = vecs_in[8:9, :] + jnp.sum(dn, axis=0, keepdims=True)
    rows = jnp.concatenate([vecs_in[:7, :], gain_row, shift_row, vecs_in[9:, :]], axis=0)
    if not last:
        vecs_out[...] = rows
        for index, value in enumerate(sums):
            sums_out[:, index * width : (index + 1) * width] = value.astype(bf16)
        return
    grad_k = 0.0
    grad_v = 0.0
    group = refs[0].shape[0]
    for index, part in enumerate(refs[:pieces]):
        span = slice(index * group, (index + 1) * group)
        grad_k = grad_k + dot(part[...], dk[span, :], TN)
        grad_v = grad_v + dot(part[...], dv[span, :], TN)
    for index, value in enumerate(sums):
        part_out(core, keep, give, index * width, value + sums_in[:, index * width : (index + 1) * width].astype(f32))
    part_out(core, keep, give, 3 * width, grad_k)
    part_out(core, keep, give, 4 * width, grad_v)
    part_out(core, keep, give, 5 * width, vector_block(rows))
    mem_own[...] = dot(dk[:count, :], wck[...], NT) + dot(dv[:count, :], wcv[...], NT)
    if others:
        mem_other[...] = (dot(dk[count:, :], wck[...], NT) + dot(dv[count:, :], wcv[...], NT)).astype(bf16)


def self_backward(step, quad, *refs):
    mg, wo, o, q, k, v, lse, ids, n1, wq, wk, wv, gain, shift = refs[:14]
    rest = list(refs[14:])
    bias, do, dqt, dk, dv = rest[-5:]
    rest = rest[:-5]
    count, columns = q.shape
    bias[...] = mask_bias(ids[...], ids[:, :count])
    do[...] = dot(mg[...].astype(bf16), wo[...], NT).astype(bf16)

    def take(span, key_grad, value_grad):
        dk[:, span] = key_grad.astype(bf16)
        dv[:, span] = value_grad.astype(bf16)

    attend_back(q, k, v, o, lse, bias, do, dqt, take, 4 * quad)
    dq = jnp.transpose(dqt[...])
    low = n1[...]
    acts = (low[:count], low, low)
    grads = (dq, dk[...], dv[...])
    sums = [dot(act, value, TN) for act, value in zip(acts, grads)]
    gain_term = 0.0
    shift_term = 0.0
    for value, grad, weight in zip(sums, grads, (wq, wk, wv)):
        weight = weight[...].astype(f32)
        column = jnp.sum(grad.astype(f32), axis=0, keepdims=True)
        gain_term = gain_term + jnp.sum(weight * (value - shift[...] * column), axis=1, keepdims=True)
        shift_term = shift_term + jnp.sum(weight * column, axis=1, keepdims=True)
    lane = lax.broadcasted_iota(jnp.int32, (low.shape[1], 128), 1)
    vec = jnp.where(lane == 0, gain_term / gain[...], jnp.where(lane == 1, shift_term, 0.0))
    if step or quad:
        vec = vec + rest.pop(0)[...]
    if step:
        before = rest.pop(0)
        sums = [value + before[:, i * columns : (i + 1) * columns].astype(f32) for i, value in enumerate(sums)]
    if step and quad:
        core, first, keep, give = rest
        for index, value in enumerate(sums):
            earlier = first[:, index * columns : (index + 1) * columns].astype(f32)
            part_out(core, keep, give, 2 * index * columns, earlier)
            part_out(core, keep, give, (2 * index + 1) * columns, value)
        part_out(core, keep, give, 6 * columns, vec)
        return
    if not step:
        own = dot(dk[:count, :], wk[...], NT) + dot(dv[:count, :], wv[...], NT) + dot(dq, wq[...], NT)
        more = dk.shape[0] > count
        other = dot(dk[count:, :], wk[...], NT) + dot(dv[count:, :], wv[...], NT) if more else None
        if quad:
            own = own + rest.pop(0)[...]
            before = rest.pop(0)
            other = other + before[...].astype(f32) if more else None
        ng_own, ng_other = rest[-2:]
        ng_own[...] = own
        if more:
            ng_other[...] = other.astype(bf16)
    sums_out, vec_out = rest[:2]
    vec_out[...] = vec
    for index, value in enumerate(sums):
        sums_out[:, index * columns : (index + 1) * columns] = value.astype(bf16)


def input_backward(parts, xa, xb, mg, ng, gain, *refs):
    received = refs[:parts]
    halves = refs[parts:]
    count = mg.shape[0]
    group = count // 2
    grad = ng[...]
    for part in received:
        grad = grad + part[...].astype(f32)
    x = jnp.concatenate([xa[:group, :], xb[:group, :]], axis=0).astype(f32)
    normal, scale = normalize(x)
    result = (mg[...] + norm_back(normal, scale, gain[...], grad)).astype(bf16)
    for half, out in enumerate(halves):
        out[...] = result[half * group : (half + 1) * group]


def call(body, outs, args, scratch=(), flops=0, name=None, blocks=None, grant=VMEM_MIB):
    moved = sum(math.prod(a.shape) * a.dtype.itemsize for a in args)
    moved += sum(math.prod(s) * jnp.dtype(d).itemsize for s, d in outs)
    blocks = blocks or {}

    def spec(index, value):
        if value.dtype == jnp.int32:
            return pl.BlockSpec(memory_space=pltpu.SMEM)
        if index in blocks:
            shape, place = blocks[index]
            return pl.BlockSpec(shape, lambda i: place)
        return pl.BlockSpec(value.shape, lambda i: (0,) * value.ndim)

    return pl.pallas_call(
        body,
        grid=(1,),
        in_specs=[spec(index, value) for index, value in enumerate(args)],
        out_specs=[pl.BlockSpec(s, lambda i, n=len(s): (0,) * n) for s, d in outs],
        out_shape=[jax.ShapeDtypeStruct(s, d) for s, d in outs],
        scratch_shapes=[pltpu.VMEM(s, d) for s, d in scratch],
        compiler_params=pltpu.CompilerParams(vmem_limit_bytes=grant * 2**20),
        cost_estimate=pl.CostEstimate(flops=int(flops), bytes_accessed=int(moved) if flops > 1 else 1, transcendentals=0),
        name=name,
    )(*args)


def local(
    inputs_one,
    inputs_two,
    memory,
    target_ids,
    memory_ids,
    cotangent_one,
    cotangent_two,
    first_gain,
    first_bias,
    self_query,
    self_key,
    self_value,
    self_output,
    second_gain,
    second_bias,
    cross_query,
    cross_key,
    cross_value,
    cross_output,
    third_gain,
    third_bias,
    inner_weight,
    inner_bias,
    outer_weight,
    outer_bias,
):
    ring = lax.axis_size("seq")
    pairs = lax.axis_size("rows") // 2
    place = lax.axis_index("seq")
    held = inputs_one.shape[0]
    group = inputs_one.shape[1]
    width = inputs_one.shape[2]
    inner = inner_weight.shape[1]
    workers = ring // held
    count = 2 * group
    length = workers * count
    pieces = 2 * workers
    grant = min(58, VMEM_MIB * max(1, length // 1024))
    others = workers - 1
    odd = place % 2

    def flat(pair, member):
        return (2 * pair + member % 2) * ring + member // 2

    def dealt(swap):
        links = []
        for pair in range(pairs):
            for core in range(2):
                for spot in range(ring):
                    row = held * core + (spot + swap) % 2
                    links.append((flat(pair, 2 * spot + core), flat(pair, row * workers + spot // 2)))
        return links

    def turned(shift):
        links = []
        for pair in range(pairs):
            for member in range(2 * ring):
                row, worker = divmod(member, workers)
                links.append((flat(pair, row * workers + (worker + shift) % workers), flat(pair, member)))
        return links

    def reverse(links):
        return [(b, a) for a, b in links]

    def send(value, links):
        return lax.ppermute(value, BOTH, links)

    def pick(value, swap):
        return lax.dynamic_index_in_dim(value, odd if swap == 0 else 1 - odd, 0, keepdims=False)

    def deal(*values):
        return [send(jnp.concatenate([pick(v, s) for v in values], axis=0), dealt(s)) for s in range(2)]

    def row_of(parts):
        whole = list(parts)
        for shift in range(1, workers):
            whole += [send(part, turned(shift)) for part in parts]
        return whole

    def back_sum(rest):
        return [
            send(rest[(shift - 1) * count : shift * count], reverse(turned(shift))) for shift in range(1, workers)
        ]

    def row(vector):
        return vector.reshape(1, -1)

    def give_back(halves):
        return [send(half, reverse(dealt(s))) for s, half in enumerate(halves)]

    def undeal(parts, step):
        parts = [part[step * group : (step + 1) * group] for part in parts]
        return jnp.where(odd == 0, jnp.stack(parts), jnp.stack(parts[::-1]))

    spot = lax.axis_index("rows")
    core = spot % 2
    bits = pairs.bit_length() - 1

    def chip_stage(turn):
        links = []
        for i in range(2 * pairs):
            links.append((i, i ^ (2 << ((turn + i % 2) % bits))))
        bit = jnp.where(core == 0, (spot >> (1 + turn % bits)) & 1, (spot >> (1 + (turn + 1) % bits)) & 1)
        return bit, links

    stages = [(core, [(i, i ^ 1) for i in range(2 * pairs)])] + [chip_stage(turn) for turn in range(bits)]

    def split(parts, stage):
        bit, links = stages[stage]
        half = parts[0].shape[0] // 2
        parts = [part.reshape((2, half) + part.shape[1:]) for part in parts]
        take = lambda i: total(*[lax.dynamic_index_in_dim(part, i, 0, keepdims=False) for part in parts])
        return take(bit), lax.ppermute(take(1 - bit), "rows", links)

    def total(first, *rest):
        result = first.astype(f32)
        for part in rest:
            result = result + part.astype(f32)
        return result.astype(bf16)

    def join_sends(value, stage):
        return [value, lax.ppermute(value, "rows", stages[stage][1])]

    def joined(parts, stage):
        value, other = parts
        bit = stages[stage][0]
        return jnp.where(bit == 0, jnp.concatenate([value, other]), jnp.concatenate([other, value]))

    def join(value, stage):
        return joined(join_sends(value, stage), stage)

    turns = ring.bit_length() - 1

    def along(value, turn):
        return [value, lax.ppermute(value, "seq", [(i, i ^ (1 << turn)) for i in range(ring)])]

    direct = {
        "core": ("rows", 2, core, [[(i, i ^ 1) for i in range(2 * pairs)]]),
        "chips": ("rows", pairs, spot // 2, [[(i, i ^ (2 * k)) for i in range(2 * pairs)] for k in range(1, pairs)]),
        "line": ("seq", ring, place, [[(i, i ^ k) for i in range(ring)] for k in range(1, ring)]),
    }

    def swap(keep, give):
        return [keep, lax.ppermute(give, "rows", stages[0][1])]

    def spread(parts, stage):
        axis, size, index, links = direct[stage]
        share = parts[0].shape[0] // size
        parts = [part.reshape((size, share) + part.shape[1:]) for part in parts]
        take = lambda i: total(*[lax.dynamic_index_in_dim(part, i, 0, keepdims=False) for part in parts])
        return [take(index)] + [lax.ppermute(take(index ^ (k + 1)), axis, link) for k, link in enumerate(links)]

    def gather_sends(value, stage):
        axis, size, index, links = direct[stage]
        return [value] + [lax.ppermute(value, axis, link) for link in links]

    def gathered(parts, stage):
        index = direct[stage][2]
        size = len(parts)
        levels = size.bit_length() - 1
        result = jnp.stack(parts).reshape((2,) * levels + parts[0].shape)
        for level in range(levels):
            result = jnp.where((index >> level) & 1 == 1, jnp.flip(result, levels - 1 - level), result)
        return result.reshape((size * parts[0].shape[0],) + parts[0].shape[1:])

    def gather(value, stage):
        return gathered(gather_sends(value, stage), stage)

    def after(values, *needed):
        return lax.optimization_barrier((values, needed))[0]

    g1, b1, g2, b2, g3, b3 = map(
        row, (first_gain, first_bias, second_gain, second_bias, third_gain, third_bias)
    )
    id_block = jnp.concatenate([target_ids, memory_ids], axis=1).astype(bf16)[:, None, :]
    id_block = jnp.pad(id_block, ((0, 0), (0, 15), (0, width - 2 * group)))
    own = deal(inputs_one, id_block)
    xs = row_of(own)
    own_memory = deal(after(memory, *xs))

    tokens = (count, width)
    whole = (length, width)
    lse = (HEADS, count)
    scores = 2 * count * length * width
    square = 2 * count * width * width

    def run_self(xs, step, *ids):
        rows = [((1, length), f32)] * 2 if step == 0 else []
        return call(
            functools.partial(self_forward, pieces, step),
            [
                (whole, bf16), (tokens, bf16), (whole, bf16), (whole, bf16), (tokens, bf16), (lse, f32), (tokens, f32),
                (tokens, bf16), *rows,
            ],
            [*xs, g1, b1, self_query, self_key, self_value, self_output, g2, b2, cross_query, *ids],
            [],
            8 * scores + (3 + 2 * workers) * square,
            "self_forward",
            grant=grant,
        )

    def run_cross(qc, mid):
        return call(
            cross_forward,
            [(tokens, bf16), (lse, f32), (tokens, f32)],
            [ids_t, ids_m, qc, mem_k, mem_v, mid, cross_output],
            [],
            8 * scores + square,
            "cross_forward",
            grant=grant,
        )

    n1_a, q_a, k_a, v_a, o_a, lse_a, mid_a, qc_a, ids_t, ids_m = run_self(xs, 0)
    mem = row_of(after(own_memory, qc_a))
    own_two = deal(after(inputs_two, *mem))
    mem_k, mem_v = call(
        functools.partial(memory_project, pieces),
        [(whole, bf16), (whole, bf16)],
        [*mem, cross_key, cross_value],
        flops=2 * workers * square,
        name="memory_project",
    )
    oc_a, lsec_a, later_a = run_cross(qc_a, mid_a)
    xs_two = row_of(after(own_two, later_a))
    cots = deal(*after((cotangent_one, cotangent_two), *xs_two))
    n1_b, q_b, k_b, v_b, o_b, lse_b, mid_b, qc_b = run_self(xs_two, 1, ids_t)
    oc_b, lsec_b, later_b = run_cross(qc_b, mid_b)
    both = (2 * count, width)
    half = width // 2
    which = jnp.reshape(core, (1,)).astype(jnp.int32)
    out_a, out_b, lg_a, lg_b, keep, give, vecs = call(
        feed_forward,
        [
            ((2 * group, width), bf16), ((2 * group, width), bf16), (tokens, f32), (tokens, f32),
            ((half, 2 * inner), bf16), ((half, 2 * inner), bf16), ((16, width), f32),
        ],
        [which, later_a, later_b, *cots, g3, b3, inner_weight, row(inner_bias), outer_weight, row(outer_bias)],
        [(both, bf16), (both, f32), (both, f32)],
        2 * 6 * square * inner // width,
        "feed_forward",
    )
    rest = (max(others, 1) * count, width)
    back_scratch = [((length, count), f32), (tokens, bf16), ((width, count), bf16)]
    ff_parts = swap(keep, give)
    back_out = give_back([out_a, out_b])
    mg_a, cross_sums, dk_a, dv_a, vecs = call(
        functools.partial(cross_backward, 0, others),
        [(tokens, f32), ((width, 3 * width), bf16), (whole, bf16), (whole, bf16), ((16, width), f32)],
        [lg_a, mid_a, oc_a, qc_a, lsec_a, o_a, mem_k, mem_v, ids_t, ids_m, cross_output, cross_query, g2, b2, vecs],
        back_scratch,
        20 * scores + 5 * square,
        "cross_backward",
        grant=58,
    )
    lg_b = after(lg_b, mg_a, *ff_parts, *back_out)
    ff_parts = split(after(ff_parts, mg_a), 1)
    mg_b, keep, give, mem_own, mem_other = call(
        functools.partial(cross_backward, pieces, others),
        [(tokens, f32), ((half, 5 * width + 128), bf16), ((half, 5 * width + 128), bf16), (tokens, f32), (rest, bf16)],
        [
            *mem, lg_b, mid_b, oc_b, qc_b, lsec_b, o_b, mem_k, mem_v, ids_t, ids_m, cross_output, cross_query,
            g2, b2, vecs, which, cross_key, cross_value, cross_sums, dk_a, dv_a,
        ],
        back_scratch + [(whole, bf16), (whole, bf16)],
        20 * scores + 14 * square,
        "cross_backward_last",
        grant=58,
    )

    def run_back(step, quad, mg, extra, outs):
        o, q, k, v, norm, lse = ((o_a, q_a, k_a, v_a, n1_a, lse_a), (o_b, q_b, k_b, v_b, n1_b, lse_b))[step]
        columns = (0, quad)
        blocks = {1: ((QUAD, width), (quad, 0))}
        blocks.update({i: ((count, QUAD), columns) for i in (2, 3)})
        blocks.update({i: ((length, QUAD), columns) for i in (4, 5)})
        blocks.update({i: ((width, QUAD), columns) for i in (9, 10, 11)})
        return call(
            functools.partial(self_backward, step, quad),
            outs,
            [
                mg, self_output, o, q, k, v, lse, ids_t, norm, self_query, self_key, self_value,
                first_gain.reshape(-1, 1), first_bias.reshape(-1, 1), *extra,
            ],
            [
                ((length, count), f32), ((count, QUAD), bf16), ((QUAD, count), bf16),
                ((length, QUAD), bf16), ((length, QUAD), bf16),
            ],
            10 * scores,
            "self_backward",
            blocks,
            grant,
        )

    sums_shape = ((width, 3 * QUAD), bf16)
    vec_shape = ((width, 128), f32)
    keep_shape = ((half, 3 * width + 128), bf16)
    mg_a = after(mg_a, mg_b, *ff_parts)
    ff_parts = split(after(ff_parts, mg_b), 2)
    for turn in range(2, bits):
        ff_parts = split(ff_parts, 1 + turn)
    cross_parts = swap(keep, give)
    memory_parts = back_sum(mem_other)
    sums_0, vec, ng_own, ng_other = run_back(0, 0, mg_a, [], [sums_shape, vec_shape, (tokens, f32), (rest, bf16)])
    mg_a = after(mg_a, vec, *ff_parts, *cross_parts, *memory_parts)
    ff_parts = spread(after(ff_parts, vec), "line")
    cross_parts = split(after(cross_parts, vec), 1)
    sums_1, vec, ng_own, ng_other = run_back(
        0, 1, mg_a, [vec, ng_own, ng_other], [sums_shape, vec_shape, (tokens, f32), (rest, bf16)]
    )
    mg_b = after(mg_b, vec, *cross_parts, *ff_parts)
    ff_parts = gather_sends(total(*after(ff_parts, vec)), "line")
    cross_parts = split(after(cross_parts, vec), 2)
    sums_0, vec = run_back(1, 0, mg_b, [vec, sums_0], [sums_shape, vec_shape])
    mg_b = after(mg_b, vec, *cross_parts, *ff_parts)
    ready = (*cross_parts, *ff_parts)
    ff_sum = gathered(after(ff_parts, vec), "line")
    for stage in reversed(range(3, 1 + bits)):
        ff_sum = join(ff_sum, stage)
    ff_parts = join_sends(ff_sum, 2)
    received = back_sum(after(ng_other, vec, *ready))
    memory_sum = after(mem_own, vec, *ready)
    for part in memory_parts:
        memory_sum = memory_sum + part.astype(f32)
    memory_sum = memory_sum.astype(bf16)
    back_memory = give_back([memory_sum[:group], memory_sum[group:]])
    cross_parts = after(cross_parts, vec)
    for turn in range(2, bits):
        cross_parts = split(cross_parts, 1 + turn)
    cross_parts = along(total(*cross_parts), 0)
    keep, give = run_back(1, 1, mg_b, [vec, sums_1, which, sums_0], [keep_shape, keep_shape])
    keep, give = after((keep, give), *ff_parts, *received)
    self_parts = swap(keep, give)
    self_parts, cross_parts = lax.optimization_barrier((self_parts, cross_parts))
    self_parts = spread(self_parts, "chips")
    ff_parts = join_sends(joined(after(ff_parts, keep), 2), 1)
    cross_parts = along(total(*after(cross_parts, keep)), 1)
    for turn in range(2, turns):
        cross_parts = along(total(*cross_parts), turn)
    halves = call(
        functools.partial(input_backward, others),
        [((group, width), bf16), ((group, width), bf16)],
        [*own, mg_a, after(ng_own, self_parts[0]), g1, *received],
        name="input_backward",
    )
    both_parts = lax.optimization_barrier((self_parts, cross_parts, ff_parts, halves, back_memory))
    halves, back_memory = both_parts[3:]
    self_parts = spread(both_parts[0], "line")
    cross_parts = join_sends(total(*both_parts[1]), bits)
    both_parts = lax.optimization_barrier((self_parts, cross_parts, both_parts[2]))
    self_parts = gather_sends(total(*both_parts[0]), "line")
    cross_sum = joined(both_parts[1], bits)
    for stage in reversed(range(2, bits)):
        cross_sum = join(cross_sum, stage)
    cross_parts = join_sends(cross_sum, 1)
    ff_parts = join_sends(joined(after(both_parts[2], self_parts[0]), 1), 0)
    both_parts = lax.optimization_barrier((self_parts, cross_parts))
    self_parts = gather_sends(gathered(both_parts[0], "line"), "chips")
    cross_parts = join_sends(joined(both_parts[1], 1), 0)
    back_input = give_back(after(halves, *both_parts[0]))
    ff_parts = after(ff_parts, *both_parts[0])

    def block(parts, index):
        return joined([part[:, index * width : (index + 1) * width] for part in parts], 0).astype(f32)

    def vectors(packed, start):
        rows = packed[: 16 * (width // 128), start : start + 128].astype(f32)
        return jnp.swapaxes(rows.reshape(width // 128, 16, 128), 0, 1).reshape(16, width)

    packed_cross = joined(cross_parts, 0)
    cross_blocks = [packed_cross[:, i * width : (i + 1) * width].astype(f32) for i in range(5)]
    inner_grad = joined([part[:, :inner] for part in ff_parts], 0).astype(f32)
    outer_grad = jnp.concatenate([block(ff_parts, inner // width + i) for i in range(inner // width)], axis=0)
    self_parts, cross_blocks, inner_grad, outer_grad, back_input = lax.optimization_barrier(
        (self_parts, cross_blocks, inner_grad, outer_grad, back_input)
    )
    packed_self = join(gathered(self_parts, "chips"), 0)

    vec = vectors(packed_cross, 5 * width)
    vec_self = packed_self[:, 3 * width : 3 * width + 2].astype(f32)
    return (
        undeal(back_out, 0),
        undeal(back_out, 1),
        undeal(back_input, 0),
        undeal(back_memory, 0),
        vec_self[:, 0],
        vec_self[:, 1],
        packed_self[:, 0 * width : 1 * width].astype(f32),
        packed_self[:, 1 * width : 2 * width].astype(f32),
        packed_self[:, 2 * width : 3 * width].astype(f32),
        cross_blocks[2],
        vec[7],
        vec[8],
        cross_blocks[1],
        cross_blocks[3],
        cross_blocks[4],
        cross_blocks[0],
        vec[0],
        vec[1],
        inner_grad,
        vec[3 : 3 + inner // width].reshape(-1),
        outer_grad,
        vec[2],
    )


def solution(mesh):
    split = P("rows", "seq", None)
    ids = P("rows", "seq")
    return jax.shard_map(
        local,
        mesh=mesh,
        in_specs=(split, split, split, ids, ids, split, split) + (P(),) * 18,
        out_specs=(split,) * 4 + (P(),) * 18,
        check_vma=False,
    )
```

```python
import functools
import math

import jax
import jax.numpy as jnp
from jax import lax
from jax.experimental import pallas as pl
from jax.experimental.pallas import tpu as pltpu
from jax.sharding import PartitionSpec as P

HEADS = 8
HEAD = 64
QUAD = 4 * HEAD
IDS = 5
VMEM_MIB = 26
epsilon = 1e-05
negative = -1e30
BOTH = ("rows", "seq")
bf16 = jnp.bfloat16
f32 = jnp.float32
LN2 = math.log(2.0)
QUERY_SCALE = HEAD ** (-0.5) / LN2
NN = ((1,), (0,))
NT = ((1,), (1,))
TN = ((0,), (0,))
GELU_A = math.sqrt(2.0 / math.pi)
GELU_B = 0.044715


def dot(left, right, dims):
    return lax.dot_general(left, right, (dims, ((), ())), preferred_element_type=f32)


def normalize(values):
    centered = values - jnp.mean(values, axis=-1, keepdims=True)
    scale = lax.rsqrt(jnp.mean(centered * centered, axis=-1, keepdims=True) + epsilon)
    return centered * scale, scale


def norm_back(normal, scale, gain, grad):
    inner = grad * gain
    mean = jnp.mean(inner, axis=-1, keepdims=True)
    along = jnp.mean(inner * normal, axis=-1, keepdims=True)
    return scale * (inner - mean - normal * along)


def mask_bias(row_ids, column_ids):
    rows = row_ids.shape[1]
    columns = column_ids.shape[1]
    spread = jnp.transpose(jnp.broadcast_to(row_ids.astype(f32), (128, rows)))
    spread = jnp.concatenate([spread] * (columns // 128), axis=1)
    return jnp.where(spread == column_ids.astype(f32), 0.0, negative)


def spread_ids(ids):
    spread = jnp.transpose(jnp.broadcast_to(ids.astype(f32), (128, ids.shape[1])))
    return jnp.concatenate([spread] * (QUAD // 128), axis=1)


def attend(q_ref, k_ref, v_ref, ids_q, ids_k, out_ref, lse_ref):
    count = q_ref.shape[0]
    length = k_ref.shape[0]
    group = lax.broadcasted_iota(jnp.int32, (count, QUAD), 1) // HEAD
    column = lax.broadcasted_iota(jnp.int32, (count, QUAD), 1) % HEAD
    group_k = lax.broadcasted_iota(jnp.int32, (length, QUAD), 1) // HEAD
    column_k = (lax.broadcasted_iota(jnp.int32, (length, QUAD), 1) % HEAD).astype(f32)
    slot = lax.broadcasted_iota(jnp.int32, (count, 128), 1)
    key_mask = jnp.where(column_k == spread_ids(ids_k), 1.0, 0.0).astype(bf16)
    seen = (column.astype(f32) == spread_ids(ids_q)) | (column >= IDS)
    query_mask = jnp.where(seen, 0.0, negative).astype(bf16)
    lse = jnp.zeros((count, 128), f32)
    for quad in range(HEADS // 4):
        span = slice(QUAD * quad, QUAD * quad + QUAD)
        queries = q_ref[:, span]
        keys = k_ref[:, span]
        values = v_ref[:, span]
        gathered = jnp.zeros((count, QUAD), f32)
        for head in range(4):
            beside = (head + 1) % 4
            own = jnp.where(group == head, queries, jnp.where(group == beside, query_mask, jnp.zeros_like(queries)))
            scores = dot(own, jnp.where(group_k == head, keys, key_mask), NT)
            top = jnp.max(scores, axis=1, keepdims=True)
            weights = jnp.exp2(scores - top).astype(bf16)
            result = dot(weights, jnp.where(group_k == head, values, jnp.ones_like(values)), NN)
            total = result[:, HEAD * beside : HEAD * beside + 1]
            gathered = jnp.where(group == head, result / total, gathered)
            lse = jnp.where(slot == 4 * quad + head, top + jnp.log2(total), lse)
        out_ref[:, span] = gathered.astype(bf16)
    lse_ref[...] = jnp.transpose(lse)[:HEADS]


def attend_back(q_ref, k_ref, v_ref, o_ref, lse_ref, bias_ref, do_ref, dqt_ref, take, base=0):
    count, columns = q_ref.shape
    lane = lax.broadcasted_iota(jnp.int32, (count, QUAD), 1) // HEAD
    product = do_ref[...].astype(f32) * o_ref[...].astype(f32)
    delta = jnp.sum(jnp.transpose(product).reshape(columns // HEAD, HEAD, count), axis=1)
    for quad in range(columns // QUAD):
        span = slice(QUAD * quad, QUAD * quad + QUAD)
        queries = q_ref[:, span]
        keys = k_ref[:, span]
        values = v_ref[:, span]
        grads = do_ref[:, span]
        keys_t = jnp.transpose(keys)
        key_grad = jnp.zeros((keys.shape[0], QUAD), f32)
        value_grad = jnp.zeros((keys.shape[0], QUAD), f32)
        for head in range(4):
            index = 4 * quad + head
            own_q = jnp.where(lane == head, queries, jnp.zeros_like(queries))
            own_g = jnp.where(lane == head, grads, jnp.zeros_like(grads))
            scores = dot(keys, own_q, NT) + bias_ref[...]
            probs = jnp.exp2(scores - lse_ref[base + index : base + index + 1, :])
            value_grad = value_grad + dot(probs.astype(bf16), own_g, NN)
            prob_grad = dot(values, own_g, NT)
            score_grad = (probs * (prob_grad - delta[index : index + 1, :])).astype(bf16)
            key_grad = key_grad + dot(score_grad, own_q, NN)
            rows = slice(HEAD * index, HEAD * index + HEAD)
            part = dot(keys_t[HEAD * head : HEAD * head + HEAD], score_grad, NN)
            dqt_ref[rows, :] = (part * HEAD ** (-0.5)).astype(bf16)
        take(span, key_grad * LN2, value_grad)


def self_forward(pieces, step, *refs):
    gain, shift, wq, wk, wv, wo, gain_two, shift_two, wcq = refs[pieces : pieces + 9]
    rest = refs[pieces + 9 :]
    if step == 0:
        n1, q, k, v, o, lse, mid, qc, ids, ids_m = rest
    else:
        ids, n1, q, k, v, o, lse, mid, qc = rest
    count = q.shape[0]
    group = count // 2
    xs = [ref.at[:group, :] for ref in refs[:pieces]]
    if step == 0:
        for index, ref in enumerate(refs[:pieces]):
            row = ref[group : group + 1, :].astype(f32)
            ids[:, index * group : (index + 1) * group] = row[:, :group]
            ids_m[:, index * group : (index + 1) * group] = row[:, group : 2 * group]
    for index, part in enumerate(xs):
        normal, _ = normalize(part[...].astype(f32))
        n1[index * group : (index + 1) * group, :] = (normal * gain[...] + shift[...]).astype(bf16)
    k[...] = dot(n1[...], wk[...], NN).astype(bf16)
    v[...] = dot(n1[...], wv[...], NN).astype(bf16)
    q[...] = (dot(n1[:count, :], wq[...], NN) * QUERY_SCALE).astype(bf16)
    attend(q, k, v, ids[:, :count], ids[...], o, lse)
    own = jnp.concatenate([part[...] for part in xs[: count // group]], axis=0).astype(f32)
    middle = own + dot(o[...], wo[...], NN)
    mid[...] = middle
    normal, _ = normalize(middle)
    low = (normal * gain_two[...] + shift_two[...]).astype(bf16)
    qc[...] = (dot(low, wcq[...], NN) * QUERY_SCALE).astype(bf16)


def memory_project(pieces, *refs):
    ms = refs[:pieces]
    wk, wv, k, v = refs[pieces:]
    group = ms[0].shape[0]
    for index, part in enumerate(ms):
        rows = slice(index * group, (index + 1) * group)
        k[rows, :] = dot(part[...], wk[...], NN).astype(bf16)
        v[rows, :] = dot(part[...], wv[...], NN).astype(bf16)


def cross_forward(ids_q, ids_k, q, k, v, mid, wo, o, lse, later):
    attend(q, k, v, ids_q[:, : q.shape[0]], ids_k[...], o, lse)
    later[...] = mid[...] + dot(o[...], wo[...], NN)


def part_out(core, keep, give, start, value):
    half, columns = value.shape[0] // 2, value.shape[1]
    value = value.astype(bf16)
    first = core[0] == 0
    keep[:, start : start + columns] = jnp.where(first, value[:half], value[half:])
    give[:, start : start + columns] = jnp.where(first, value[half:], value[:half])


def feed_forward(core, later_a, later_b, cot_a, cot_b, gain, shift, win, bin_, wout, bout, out_a, out_b, grad_a, grad_b, keep, give, vecs, cot, acc, dnorm):
    count = later_a.shape[0]
    width = later_a.shape[1]
    inner = win.shape[1]
    group = count // 2
    for step in range(2):
        for half, part in enumerate((cot_a, cot_b)):
            start = (2 * step + half) * group
            cot[start : start + group, :] = part[step * group : (step + 1) * group, :]
    later = jnp.concatenate([later_a[...], later_b[...]], axis=0)
    normal, scale = normalize(later)
    low = (normal * gain[...] + shift[...]).astype(bf16)
    bias_rows = []
    for index in range(inner // width):
        span = slice(index * width, (index + 1) * width)
        pre = dot(low, win[:, span], NN) + bin_[:, span]
        square = pre * pre
        tanh = jnp.tanh(GELU_A * (pre + GELU_B * (pre * square)))
        half = 0.5 * (1.0 + tanh)
        hidden = (pre * half).astype(bf16)
        slope = half + 0.5 * pre * (1.0 - tanh * tanh) * (GELU_A + (3.0 * GELU_A * GELU_B) * square)
        step = dot(hidden, wout[span, :], NN)
        hidden_grad = dot(cot[...], wout[span, :], NT)
        pre_grad = hidden_grad * slope
        pre_low = pre_grad.astype(bf16)
        bias_rows.append(jnp.sum(pre_grad, axis=0, keepdims=True))
        part_out(core, keep, give, index * width, dot(low, pre_low, TN))
        part_out(core, keep, give, inner + index * width, dot(hidden, cot[...], TN))
        back = dot(pre_low, win[:, span], NT)
        if index == 0:
            acc[...] = step
            dnorm[...] = back
        else:
            acc[...] = acc[...] + step
            dnorm[...] = dnorm[...] + back
    result = (later + acc[...] + bout[...]).astype(bf16)
    for half, out in enumerate((out_a, out_b)):
        for step in range(2):
            start = (2 * step + half) * group
            out[step * group : (step + 1) * group, :] = result[start : start + group]
    dn = dnorm[...]
    cots = cot[...].astype(f32)
    grad = cots + norm_back(normal, scale, gain[...], dn)
    grad_a[...] = grad[:count]
    grad_b[...] = grad[count:]
    rows = [
        jnp.sum(dn * normal, axis=0, keepdims=True),
        jnp.sum(dn, axis=0, keepdims=True),
        jnp.sum(cots, axis=0, keepdims=True),
    ] + bias_rows
    rows.append(jnp.zeros((16 - len(rows), width), f32))
    vecs[...] = jnp.concatenate(rows, axis=0)


def vector_block(rows):
    width = rows.shape[1]
    parts = [rows[:, 128 * block : 128 * block + 128] for block in range(width // 128)]
    return jnp.concatenate(parts + [jnp.zeros((width - 16 * (width // 128), 128), f32)], axis=0)


def cross_backward(pieces, others, *refs):
    last = pieces > 0
    grad, mid, oc, qc, lse, os_, k, v, ids_q, ids_k, wco, wcq, gain, shift, vecs_in = refs[pieces : pieces + 15]
    rest = refs[pieces + 15 :]
    if last:
        core, wck, wcv, sums_in, dk_in, dv_in, mg, keep, give, mem_own, mem_other, bias, do, dqt, dk, dv = rest
    else:
        mg, sums_out, dk, dv, vecs_out, bias, do, dqt = rest
    width = k.shape[1]
    count = qc.shape[0]
    bias[...] = mask_bias(ids_k[...], ids_q[:, :count])
    branch = grad[...].astype(bf16)
    do[...] = dot(branch, wco[...], NT).astype(bf16)

    def take(span, key_grad, value_grad):
        if last:
            key_grad = key_grad + dk_in[:, span].astype(f32)
            value_grad = value_grad + dv_in[:, span].astype(f32)
        dk[:, span] = key_grad.astype(bf16)
        dv[:, span] = value_grad.astype(bf16)

    attend_back(qc, k, v, oc, lse, bias, do, dqt, take)
    dq = jnp.transpose(dqt[...])
    normal, scale = normalize(mid[...])
    low = (normal * gain[...] + shift[...]).astype(bf16)
    dn = dot(dq, wcq[...], NT)
    middle_grad = grad[...] + norm_back(normal, scale, gain[...], dn)
    mg[...] = middle_grad
    sums = [dot(oc[...], branch, TN), dot(low, dq, TN), dot(os_[...], middle_grad.astype(bf16), TN)]
    gain_row = vecs_in[7:8, :] + jnp.sum(dn * normal, axis=0, keepdims=True)
    shift_row = vecs_in[8:9, :] + jnp.sum(dn, axis=0, keepdims=True)
    rows = jnp.concatenate([vecs_in[:7, :], gain_row, shift_row, vecs_in[9:, :]], axis=0)
    if not last:
        vecs_out[...] = rows
        for index, value in enumerate(sums):
            sums_out[:, index * width : (index + 1) * width] = value.astype(bf16)
        return
    grad_k = 0.0
    grad_v = 0.0
    group = refs[0].shape[0]
    for index, part in enumerate(refs[:pieces]):
        span = slice(index * group, (index + 1) * group)
        grad_k = grad_k + dot(part[...], dk[span, :], TN)
        grad_v = grad_v + dot(part[...], dv[span, :], TN)
    for index, value in enumerate(sums):
        part_out(core, keep, give, index * width, value + sums_in[:, index * width : (index + 1) * width].astype(f32))
    part_out(core, keep, give, 3 * width, grad_k)
    part_out(core, keep, give, 4 * width, grad_v)
    part_out(core, keep, give, 5 * width, vector_block(rows))
    mem_own[...] = dot(dk[:count, :], wck[...], NT) + dot(dv[:count, :], wcv[...], NT)
    if others:
        mem_other[...] = (dot(dk[count:, :], wck[...], NT) + dot(dv[count:, :], wcv[...], NT)).astype(bf16)


def self_backward(step, quad, *refs):
    mg, wo, o, q, k, v, lse, ids, n1, wq, wk, wv, gain, shift = refs[:14]
    rest = list(refs[14:])
    bias, do, dqt, dk, dv = rest[-5:]
    rest = rest[:-5]
    count, columns = q.shape
    bias[...] = mask_bias(ids[...], ids[:, :count])
    do[...] = dot(mg[...].astype(bf16), wo[...], NT).astype(bf16)

    def take(span, key_grad, value_grad):
        dk[:, span] = key_grad.astype(bf16)
        dv[:, span] = value_grad.astype(bf16)

    attend_back(q, k, v, o, lse, bias, do, dqt, take, 4 * quad)
    dq = jnp.transpose(dqt[...])
    low = n1[...]
    acts = (low[:count], low, low)
    grads = (dq, dk[...], dv[...])
    sums = [dot(act, value, TN) for act, value in zip(acts, grads)]
    gain_term = 0.0
    shift_term = 0.0
    for value, grad, weight in zip(sums, grads, (wq, wk, wv)):
        weight = weight[...].astype(f32)
        column = jnp.sum(grad.astype(f32), axis=0, keepdims=True)
        gain_term = gain_term + jnp.sum(weight * (value - shift[...] * column), axis=1, keepdims=True)
        shift_term = shift_term + jnp.sum(weight * column, axis=1, keepdims=True)
    lane = lax.broadcasted_iota(jnp.int32, (low.shape[1], 128), 1)
    vec = jnp.where(lane == 0, gain_term / gain[...], jnp.where(lane == 1, shift_term, 0.0))
    if step or quad:
        vec = vec + rest.pop(0)[...]
    if step:
        before = rest.pop(0)
        sums = [value + before[:, i * columns : (i + 1) * columns].astype(f32) for i, value in enumerate(sums)]
    if step and quad:
        core, first, keep, give = rest
        for index, value in enumerate(sums):
            earlier = first[:, index * columns : (index + 1) * columns].astype(f32)
            part_out(core, keep, give, 2 * index * columns, earlier)
            part_out(core, keep, give, (2 * index + 1) * columns, value)
        part_out(core, keep, give, 6 * columns, vec)
        return
    if not step:
        own = dot(dk[:count, :], wk[...], NT) + dot(dv[:count, :], wv[...], NT) + dot(dq, wq[...], NT)
        more = dk.shape[0] > count
        other = dot(dk[count:, :], wk[...], NT) + dot(dv[count:, :], wv[...], NT) if more else None
        if quad:
            own = own + rest.pop(0)[...]
            before = rest.pop(0)
            other = other + before[...].astype(f32) if more else None
        ng_own, ng_other = rest[-2:]
        ng_own[...] = own
        if more:
            ng_other[...] = other.astype(bf16)
    sums_out, vec_out = rest[:2]
    vec_out[...] = vec
    for index, value in enumerate(sums):
        sums_out[:, index * columns : (index + 1) * columns] = value.astype(bf16)


def input_backward(parts, xa, xb, mg, ng, gain, *refs):
    received = refs[:parts]
    halves = refs[parts:]
    count = mg.shape[0]
    group = count // 2
    grad = ng[...]
    for part in received:
        grad = grad + part[...].astype(f32)
    x = jnp.concatenate([xa[:group, :], xb[:group, :]], axis=0).astype(f32)
    normal, scale = normalize(x)
    result = (mg[...] + norm_back(normal, scale, gain[...], grad)).astype(bf16)
    for half, out in enumerate(halves):
        out[...] = result[half * group : (half + 1) * group]


def call(body, outs, args, scratch=(), flops=0, name=None, blocks=None, grant=VMEM_MIB):
    moved = sum(math.prod(a.shape) * a.dtype.itemsize for a in args)
    moved += sum(math.prod(s) * jnp.dtype(d).itemsize for s, d in outs)
    blocks = blocks or {}

    def spec(index, value):
        if value.dtype == jnp.int32:
            return pl.BlockSpec(memory_space=pltpu.SMEM)
        if index in blocks:
            shape, place = blocks[index]
            return pl.BlockSpec(shape, lambda i: place)
        return pl.BlockSpec(value.shape, lambda i: (0,) * value.ndim)

    return pl.pallas_call(
        body,
        grid=(1,),
        in_specs=[spec(index, value) for index, value in enumerate(args)],
        out_specs=[pl.BlockSpec(s, lambda i, n=len(s): (0,) * n) for s, d in outs],
        out_shape=[jax.ShapeDtypeStruct(s, d) for s, d in outs],
        scratch_shapes=[pltpu.VMEM(s, d) for s, d in scratch],
        compiler_params=pltpu.CompilerParams(vmem_limit_bytes=grant * 2**20),
        cost_estimate=pl.CostEstimate(flops=int(flops), bytes_accessed=int(moved) if flops > 1 else 1, transcendentals=0),
        name=name,
    )(*args)


def local(
    inputs_one,
    inputs_two,
    memory,
    target_ids,
    memory_ids,
    cotangent_one,
    cotangent_two,
    first_gain,
    first_bias,
    self_query,
    self_key,
    self_value,
    self_output,
    second_gain,
    second_bias,
    cross_query,
    cross_key,
    cross_value,
    cross_output,
    third_gain,
    third_bias,
    inner_weight,
    inner_bias,
    outer_weight,
    outer_bias,
):
    ring = lax.axis_size("seq")
    pairs = lax.axis_size("rows") // 2
    place = lax.axis_index("seq")
    held = inputs_one.shape[0]
    group = inputs_one.shape[1]
    width = inputs_one.shape[2]
    inner = inner_weight.shape[1]
    workers = ring // held
    count = 2 * group
    length = workers * count
    pieces = 2 * workers
    grant = min(58, VMEM_MIB * max(1, length // 1024))
    others = workers - 1
    odd = place % 2

    def flat(pair, member):
        return (2 * pair + member % 2) * ring + member // 2

    def dealt(swap):
        links = []
        for pair in range(pairs):
            for core in range(2):
                for spot in range(ring):
                    row = held * core + (spot + swap) % 2
                    links.append((flat(pair, 2 * spot + core), flat(pair, row * workers + spot // 2)))
        return links

    def turned(shift):
        links = []
        for pair in range(pairs):
            for member in range(2 * ring):
                row, worker = divmod(member, workers)
                links.append((flat(pair, row * workers + (worker + shift) % workers), flat(pair, member)))
        return links

    def reverse(links):
        return [(b, a) for a, b in links]

    def send(value, links):
        return lax.ppermute(value, BOTH, links)

    def pick(value, swap):
        return lax.dynamic_index_in_dim(value, odd if swap == 0 else 1 - odd, 0, keepdims=False)

    def deal(*values):
        return [send(jnp.concatenate([pick(v, s) for v in values], axis=0), dealt(s)) for s in range(2)]

    def row_of(parts):
        whole = list(parts)
        for shift in range(1, workers):
            whole += [send(part, turned(shift)) for part in parts]
        return whole

    def back_sum(rest):
        return [
            send(rest[(shift - 1) * count : shift * count], reverse(turned(shift))) for shift in range(1, workers)
        ]

    def row(vector):
        return vector.reshape(1, -1)

    def give_back(halves):
        return [send(half, reverse(dealt(s))) for s, half in enumerate(halves)]

    def undeal(parts, step):
        parts = [part[step * group : (step + 1) * group] for part in parts]
        return jnp.where(odd == 0, jnp.stack(parts), jnp.stack(parts[::-1]))

    spot = lax.axis_index("rows")
    core = spot % 2
    bits = pairs.bit_length() - 1

    def chip_stage(turn):
        links = []
        for i in range(2 * pairs):
            links.append((i, i ^ (2 << ((turn + i % 2) % bits))))
        bit = jnp.where(core == 0, (spot >> (1 + turn % bits)) & 1, (spot >> (1 + (turn + 1) % bits)) & 1)
        return bit, links

    stages = [(core, [(i, i ^ 1) for i in range(2 * pairs)])] + [chip_stage(turn) for turn in range(bits)]

    def split(parts, stage):
        bit, links = stages[stage]
        half = parts[0].shape[0] // 2
        parts = [part.reshape((2, half) + part.shape[1:]) for part in parts]
        take = lambda i: total(*[lax.dynamic_index_in_dim(part, i, 0, keepdims=False) for part in parts])
        return take(bit), lax.ppermute(take(1 - bit), "rows", links)

    def total(first, *rest):
        result = first.astype(f32)
        for part in rest:
            result = result + part.astype(f32)
        return result.astype(bf16)

    def join_sends(value, stage):
        return [value, lax.ppermute(value, "rows", stages[stage][1])]

    def joined(parts, stage):
        value, other = parts
        bit = stages[stage][0]
        return jnp.where(bit == 0, jnp.concatenate([value, other]), jnp.concatenate([other, value]))

    def join(value, stage):
        return joined(join_sends(value, stage), stage)

    turns = ring.bit_length() - 1

    def along(value, turn):
        return [value, lax.ppermute(value, "seq", [(i, i ^ (1 << turn)) for i in range(ring)])]

    direct = {
        "core": ("rows", 2, core, [[(i, i ^ 1) for i in range(2 * pairs)]]),
        "chips": ("rows", pairs, spot // 2, [[(i, i ^ (2 * k)) for i in range(2 * pairs)] for k in range(1, pairs)]),
        "line": ("seq", ring, place, [[(i, i ^ k) for i in range(ring)] for k in range(1, ring)]),
    }

    def swap(keep, give):
        return [keep, lax.ppermute(give, "rows", stages[0][1])]

    def spread(parts, stage):
        axis, size, index, links = direct[stage]
        share = parts[0].shape[0] // size
        parts = [part.reshape((size, share) + part.shape[1:]) for part in parts]
        take = lambda i: total(*[lax.dynamic_index_in_dim(part, i, 0, keepdims=False) for part in parts])
        return [take(index)] + [lax.ppermute(take(index ^ (k + 1)), axis, link) for k, link in enumerate(links)]

    def gather_sends(value, stage):
        axis, size, index, links = direct[stage]
        return [value] + [lax.ppermute(value, axis, link) for link in links]

    def gathered(parts, stage):
        index = direct[stage][2]
        size = len(parts)
        levels = size.bit_length() - 1
        result = jnp.stack(parts).reshape((2,) * levels + parts[0].shape)
        for level in range(levels):
            result = jnp.where((index >> level) & 1 == 1, jnp.flip(result, levels - 1 - level), result)
        return result.reshape((size * parts[0].shape[0],) + parts[0].shape[1:])

    def gather(value, stage):
        return gathered(gather_sends(value, stage), stage)

    def after(values, *needed):
        return lax.optimization_barrier((values, needed))[0]

    g1, b1, g2, b2, g3, b3 = map(
        row, (first_gain, first_bias, second_gain, second_bias, third_gain, third_bias)
    )
    id_block = jnp.concatenate([target_ids, memory_ids], axis=1).astype(bf16)[:, None, :]
    id_block = jnp.pad(id_block, ((0, 0), (0, 15), (0, width - 2 * group)))
    own = deal(inputs_one, id_block)
    xs = row_of(own)
    own_memory = deal(after(memory, *xs))

    tokens = (count, width)
    whole = (length, width)
    lse = (HEADS, count)
    scores = 2 * count * length * width
    square = 2 * count * width * width

    def run_self(xs, step, *ids):
        rows = [((1, length), f32)] * 2 if step == 0 else []
        return call(
            functools.partial(self_forward, pieces, step),
            [
                (whole, bf16), (tokens, bf16), (whole, bf16), (whole, bf16), (tokens, bf16), (lse, f32), (tokens, f32),
                (tokens, bf16), *rows,
            ],
            [*xs, g1, b1, self_query, self_key, self_value, self_output, g2, b2, cross_query, *ids],
            [],
            8 * scores + (3 + 2 * workers) * square,
            "self_forward",
            grant=grant,
        )

    def run_cross(qc, mid):
        return call(
            cross_forward,
            [(tokens, bf16), (lse, f32), (tokens, f32)],
            [ids_t, ids_m, qc, mem_k, mem_v, mid, cross_output],
            [],
            8 * scores + square,
            "cross_forward",
            grant=grant,
        )

    n1_a, q_a, k_a, v_a, o_a, lse_a, mid_a, qc_a, ids_t, ids_m = run_self(xs, 0)
    mem = row_of(after(own_memory, qc_a))
    own_two = deal(after(inputs_two, *mem))
    mem_k, mem_v = call(
        functools.partial(memory_project, pieces),
        [(whole, bf16), (whole, bf16)],
        [*mem, cross_key, cross_value],
        flops=2 * workers * square,
        name="memory_project",
    )
    oc_a, lsec_a, later_a = run_cross(qc_a, mid_a)
    xs_two = row_of(after(own_two, later_a))
    cots = deal(*after((cotangent_one, cotangent_two), *xs_two))
    n1_b, q_b, k_b, v_b, o_b, lse_b, mid_b, qc_b = run_self(xs_two, 1, ids_t)
    oc_b, lsec_b, later_b = run_cross(qc_b, mid_b)
    both = (2 * count, width)
    half = width // 2
    which = jnp.reshape(core, (1,)).astype(jnp.int32)
    out_a, out_b, lg_a, lg_b, keep, give, vecs = call(
        feed_forward,
        [
            ((2 * group, width), bf16), ((2 * group, width), bf16), (tokens, f32), (tokens, f32),
            ((half, 2 * inner), bf16), ((half, 2 * inner), bf16), ((16, width), f32),
        ],
        [which, later_a, later_b, *cots, g3, b3, inner_weight, row(inner_bias), outer_weight, row(outer_bias)],
        [(both, bf16), (both, f32), (both, f32)],
        2 * 6 * square * inner // width,
        "feed_forward",
    )
    rest = (max(others, 1) * count, width)
    back_scratch = [((length, count), f32), (tokens, bf16), ((width, count), bf16)]
    ff_parts = swap(keep, give)
    back_out = give_back([out_a, out_b])
    mg_a, cross_sums, dk_a, dv_a, vecs = call(
        functools.partial(cross_backward, 0, others),
        [(tokens, f32), ((width, 3 * width), bf16), (whole, bf16), (whole, bf16), ((16, width), f32)],
        [lg_a, mid_a, oc_a, qc_a, lsec_a, o_a, mem_k, mem_v, ids_t, ids_m, cross_output, cross_query, g2, b2, vecs],
        back_scratch,
        20 * scores + 5 * square,
        "cross_backward",
        grant=58,
    )
    lg_b = after(lg_b, mg_a, *ff_parts, *back_out)
    ff_parts = split(after(ff_parts, mg_a), 1)
    mg_b, keep, give, mem_own, mem_other = call(
        functools.partial(cross_backward, pieces, others),
        [(tokens, f32), ((half, 5 * width + 128), bf16), ((half, 5 * width + 128), bf16), (tokens, f32), (rest, bf16)],
        [
            *mem, lg_b, mid_b, oc_b, qc_b, lsec_b, o_b, mem_k, mem_v, ids_t, ids_m, cross_output, cross_query,
            g2, b2, vecs, which, cross_key, cross_value, cross_sums, dk_a, dv_a,
        ],
        back_scratch + [(whole, bf16), (whole, bf16)],
        20 * scores + 14 * square,
        "cross_backward_last",
        grant=58,
    )

    def run_back(step, quad, mg, extra, outs):
        o, q, k, v, norm, lse = ((o_a, q_a, k_a, v_a, n1_a, lse_a), (o_b, q_b, k_b, v_b, n1_b, lse_b))[step]
        columns = (0, quad)
        blocks = {1: ((QUAD, width), (quad, 0))}
        blocks.update({i: ((count, QUAD), columns) for i in (2, 3)})
        blocks.update({i: ((length, QUAD), columns) for i in (4, 5)})
        blocks.update({i: ((width, QUAD), columns) for i in (9, 10, 11)})
        return call(
            functools.partial(self_backward, step, quad),
            outs,
            [
                mg, self_output, o, q, k, v, lse, ids_t, norm, self_query, self_key, self_value,
                first_gain.reshape(-1, 1), first_bias.reshape(-1, 1), *extra,
            ],
            [
                ((length, count), f32), ((count, QUAD), bf16), ((QUAD, count), bf16),
                ((length, QUAD), bf16), ((length, QUAD), bf16),
            ],
            10 * scores,
            "self_backward",
            blocks,
            grant if step + quad else 58,
        )

    sums_shape = ((width, 3 * QUAD), bf16)
    vec_shape = ((width, 128), f32)
    keep_shape = ((half, 3 * width + 128), bf16)
    mg_a = after(mg_a, mg_b, *ff_parts)
    ff_parts = split(after(ff_parts, mg_b), 2)
    for turn in range(2, bits):
        ff_parts = split(ff_parts, 1 + turn)
    cross_parts = swap(keep, give)
    memory_parts = back_sum(mem_other)
    sums_0, vec, ng_own, ng_other = run_back(0, 0, mg_a, [], [sums_shape, vec_shape, (tokens, f32), (rest, bf16)])
    mg_a = after(mg_a, vec, *ff_parts, *cross_parts, *memory_parts)
    ff_parts = spread(after(ff_parts, vec), "line")
    cross_parts = split(after(cross_parts, vec), 1)
    sums_1, vec, ng_own, ng_other = run_back(
        0, 1, mg_a, [vec, ng_own, ng_other], [sums_shape, vec_shape, (tokens, f32), (rest, bf16)]
    )
    mg_b = after(mg_b, vec, *cross_parts, *ff_parts)
    ff_parts = gather_sends(total(*after(ff_parts, vec)), "line")
    cross_parts = split(after(cross_parts, vec), 2)
    sums_0, vec = run_back(1, 0, mg_b, [vec, sums_0], [sums_shape, vec_shape])
    mg_b = after(mg_b, vec, *cross_parts, *ff_parts)
    ready = (*cross_parts, *ff_parts)
    ff_sum = gathered(after(ff_parts, vec), "line")
    for stage in reversed(range(3, 1 + bits)):
        ff_sum = join(ff_sum, stage)
    ff_parts = join_sends(ff_sum, 2)
    received = back_sum(after(ng_other, vec, *ready))
    memory_sum = after(mem_own, vec, *ready)
    for part in memory_parts:
        memory_sum = memory_sum + part.astype(f32)
    memory_sum = memory_sum.astype(bf16)
    back_memory = give_back([memory_sum[:group], memory_sum[group:]])
    cross_parts = after(cross_parts, vec)
    for turn in range(2, bits):
        cross_parts = split(cross_parts, 1 + turn)
    cross_parts = along(total(*cross_parts), 0)
    keep, give = run_back(1, 1, mg_b, [vec, sums_1, which, sums_0], [keep_shape, keep_shape])
    keep, give = after((keep, give), *ff_parts, *received)
    self_parts = swap(keep, give)
    self_parts, cross_parts = lax.optimization_barrier((self_parts, cross_parts))
    self_parts = spread(self_parts, "chips")
    ff_parts = join_sends(joined(after(ff_parts, keep), 2), 1)
    cross_parts = along(total(*after(cross_parts, keep)), 1)
    for turn in range(2, turns):
        cross_parts = along(total(*cross_parts), turn)
    halves = call(
        functools.partial(input_backward, others),
        [((group, width), bf16), ((group, width), bf16)],
        [*own, mg_a, after(ng_own, self_parts[0]), g1, *received],
        name="input_backward",
    )
    both_parts = lax.optimization_barrier((self_parts, cross_parts, ff_parts, halves, back_memory))
    halves, back_memory = both_parts[3:]
    self_parts = spread(both_parts[0], "line")
    cross_parts = join_sends(total(*both_parts[1]), bits)
    both_parts = lax.optimization_barrier((self_parts, cross_parts, both_parts[2]))
    self_parts = gather_sends(total(*both_parts[0]), "line")
    cross_sum = joined(both_parts[1], bits)
    for stage in reversed(range(2, bits)):
        cross_sum = join(cross_sum, stage)
    cross_parts = join_sends(cross_sum, 1)
    ff_parts = join_sends(joined(after(both_parts[2], self_parts[0]), 1), 0)
    both_parts = lax.optimization_barrier((self_parts, cross_parts))
    self_parts = gather_sends(gathered(both_parts[0], "line"), "chips")
    cross_parts = join_sends(joined(both_parts[1], 1), 0)
    back_input = give_back(after(halves, *both_parts[0]))
    ff_parts = after(ff_parts, *both_parts[0])

    def block(parts, index):
        return joined([part[:, index * width : (index + 1) * width] for part in parts], 0).astype(f32)

    def vectors(packed, start):
        rows = packed[: 16 * (width // 128), start : start + 128].astype(f32)
        return jnp.swapaxes(rows.reshape(width // 128, 16, 128), 0, 1).reshape(16, width)

    packed_cross = joined(cross_parts, 0)
    cross_blocks = [packed_cross[:, i * width : (i + 1) * width].astype(f32) for i in range(5)]
    inner_grad = joined([part[:, :inner] for part in ff_parts], 0).astype(f32)
    outer_grad = jnp.concatenate([block(ff_parts, inner // width + i) for i in range(inner // width)], axis=0)
    self_parts, cross_blocks, inner_grad, outer_grad, back_input = lax.optimization_barrier(
        (self_parts, cross_blocks, inner_grad, outer_grad, back_input)
    )
    packed_self = join(gathered(self_parts, "chips"), 0)

    vec = vectors(packed_cross, 5 * width)
    vec_self = packed_self[:, 3 * width : 3 * width + 2].astype(f32)
    return (
        undeal(back_out, 0),
        undeal(back_out, 1),
        undeal(back_input, 0),
        undeal(back_memory, 0),
        vec_self[:, 0],
        vec_self[:, 1],
        packed_self[:, 0 * width : 1 * width].astype(f32),
        packed_self[:, 1 * width : 2 * width].astype(f32),
        packed_self[:, 2 * width : 3 * width].astype(f32),
        cross_blocks[2],
        vec[7],
        vec[8],
        cross_blocks[1],
        cross_blocks[3],
        cross_blocks[4],
        cross_blocks[0],
        vec[0],
        vec[1],
        inner_grad,
        vec[3 : 3 + inner // width].reshape(-1),
        outer_grad,
        vec[2],
    )


def solution(mesh):
    split = P("rows", "seq", None)
    ids = P("rows", "seq")
    return jax.shard_map(
        local,
        mesh=mesh,
        in_specs=(split, split, split, ids, ids, split, split) + (P(),) * 18,
        out_specs=(split,) * 4 + (P(),) * 18,
        check_vma=False,
    )
```
